32 devices in a mesh: rows: 16 (over z, y, core), chan: 2 (over x).
Axes of the slice: x: 2, y: 2, z: 4, core: 2. Of those that a mesh axis runs over, the one named last changes fastest.
Arguments:
- features: bfloat16 [128, 256, 2048], P('rows', None, 'chan'), may hold values from -6 to 6
- grad_out: bfloat16 [3, 128, 256, 256], P(None, 'rows', 'chan'), may hold values from -6 to 6
- pre_act: bfloat16 [3, 128, 256, 256], P(None, 'rows', 'chan'), may hold values from -6 to 6
- weights: bfloat16 [3, 9, 256, 2048], P(None, None, None, 'chan'), may hold values from -0.046875 to 0.046875
Outputs:
- grad_input: bfloat16 [128, 256, 2048], P('rows', None, 'chan')
- grad_weight: float32 [3, 9, 256, 2048], P(None, None, 'rows', 'chan')
The draws below stay inside these ranges and needn't reach their ends.
All inputs are finite; a program needn't handle non-finite values.
Results may differ from the reference program's by a relative error of at most 0.001.
Values may be sent and summed in bfloat16 or wider, within the bound.
No kernel may reach another device: no remote copies, remote signals or barrier semaphores. Data moves between devices by JAX's collectives and lax.ppermute only.
A program may use at most 192 MiB of HBM per device.

```python
import jax
import jax.numpy as jnp

C = 2048
COUT = 256
RATE_A = 12
RATE_B = 24
RATE_C = 36
COLS = 256
H = 128


def strengthened(drawn, stream_key, source, target, shards_of, factor):
    owner, partner = [(jnp.arange(drawn.shape[dim]) // (drawn.shape[dim] // shards_of)).reshape([-1 if axis == dim else 1 for axis in range(drawn.ndim)]) for dim in (source, target)]
    chosen = jax.random.permutation(stream_key, shards_of)[partner]
    strong = (owner == chosen) | (owner == (partner + shards_of // 2) % shards_of)
    return jnp.where(strong, factor * drawn, drawn)


def levels(rng, extent, split, low, top_value):
    level = 1.0
    for position, parts in split:
        heights = jax.random.uniform(jax.random.fold_in(jax.random.fold_in(rng, 6), position), (parts,), jnp.float32, low / len(split), top_value / len(split))
        level = level * jnp.repeat(jnp.exp(heights), extent[position] // parts).reshape((-1,) + (1,) * (len(extent) - 1 - position))
    return level


def centred(stream_key, dims, deviation, bound, cuts=(), held_as=jnp.bfloat16):
    entries = deviation * jax.random.normal(stream_key, dims, jnp.float32)
    if cuts:
        entries = entries * levels(stream_key, dims, cuts, -0.22, 0.18)
    return jnp.clip(entries, -bound, bound).astype(held_as)


def noise_with(stream_key, dims, spread, bound, cuts, heavy, dtype=jnp.bfloat16):
    result = spread * jax.random.normal(stream_key, dims, jnp.float32)
    if cuts:
        result = result * levels(stream_key, dims, cuts, -0.22, 0.18)
    return jnp.clip(strengthened(result, jax.random.fold_in(stream_key, 3), *heavy), -bound, bound).astype(dtype)


def setup_inputs(seed: int = 0) -> dict:
    splits = jax.random.split(jax.random.key(seed), 5)
    return {
        "features": centred(splits[0], (H, COLS, C), 1.0, 6.0, ((0, 16), (2, 2))),
        "grad_out": noise_with(splits[1], (3, H, COUT, COLS), 1.0, 6.0, ((1, 16), (2, 2)), (1, 2, 16, 2.0)),
        "pre_act": centred(splits[2], (3, H, COUT, COLS), 1.0, 6.0, ((1, 16), (2, 2))),
        "weights": centred(splits[3], (3, 9, COUT, C), (9 * C) ** -0.5, 0.046875, ((3, 2),)),
    }


grad_scale = 0.00390625


def shifted_field(field, row_step, col_step, dilation):
    padded = jnp.pad(field, ((dilation, dilation), (0, 0), (dilation, dilation)))
    rows_at = dilation - row_step * dilation
    cols_at = dilation - col_step * dilation
    return padded[rows_at:rows_at + H, :, cols_at:cols_at + COLS]


def reference(features, grad_out, pre_act, weights):
    masked = grad_out * (pre_act > 0).astype(jnp.bfloat16)
    feat_wide = features.astype(jnp.float32)
    grad_input = jnp.zeros((H, COLS, C), jnp.float32)
    kernel_list = []
    for branch, dilation in enumerate((RATE_A, RATE_B, RATE_C)):
        tap_list = []
        for row_step in (-1, 0, 1):
            for col_step in (-1, 0, 1):
                tap_index = (row_step + 1) * 3 + (col_step + 1)
                moved = shifted_field(masked[branch], row_step, col_step, dilation).astype(jnp.float32)
                kernel = weights[branch, tap_index].astype(jnp.float32)
                grad_input = grad_input + jnp.einsum('hoc,oi->hci', moved, kernel)
                tap_list.append(jnp.einsum('hoc,hci->oi', moved, feat_wide))
        kernel_list.append(jnp.stack(tap_list, axis=0))
    grad_weight = jnp.stack(kernel_list, axis=0) * grad_scale
    return grad_input.astype(jnp.bfloat16), grad_weight
```

```python
import functools

import jax
import jax.numpy as jnp
from jax import lax
from jax.experimental import pallas as pl
from jax.experimental.pallas import tpu as pltpu
from jax.sharding import PartitionSpec as P

RATES = (12, 24, 36)
grad_scale = 0.00390625
SHARED = (0, 1, 2)


def passed_along(array, axis, by):
    count = lax.axis_size(axis)
    pairs = [(i, i + by) for i in range(count) if 0 <= i + by < count]
    return lax.ppermute(array, axis, pairs)


def swapped(array, axis, bit):
    count = lax.axis_size(axis)
    return lax.ppermute(array, axis, [(i, i ^ bit) for i in range(count)])


def row_pieces(dilation, side, rows_dev):
    start_strip = side * dilation // rows_dev
    remainder = side * dilation % rows_dev
    if remainder == 0:
        return [(start_strip, 0, rows_dev)]
    return [(start_strip, remainder, rows_dev), (start_strip + 1, 0, remainder)]


def fetch(source, side, dilation):
    parts = [
        passed_along(source[low:high], "rows", -strip)
        for strip, low, high in row_pieces(dilation, side, source.shape[0])
    ]
    return parts[0] if len(parts) == 1 else jnp.concatenate(parts, axis=0)


def moved(tile, shift):
    if shift == 0:
        return tile
    cols = tile.shape[-1]
    col = lax.broadcasted_iota(jnp.int32, tile.shape, 1)
    keep = col >= shift if shift > 0 else col < cols + shift
    return jnp.where(keep, pltpu.roll(tile, shift % cols, 1), jnp.zeros_like(tile))


def kernel_grad_body(dilation, core_ref, upper, own, lower, feats_hbm, keep_hbm, send_hbm,
                     feats, taps_a, taps_b, sums, feat_sem, out_sems):
    rows_dev, groups, _, lanes, cols = own.shape
    half = groups * lanes
    core = core_ref[0]
    load = pltpu.make_async_copy(feats_hbm, feats, feat_sem)
    load.start()
    taps = (taps_a, taps_b)

    def build(source, target):
        for row in range(rows_dev):
            for part in range(2):
                for group in range(groups):
                    tile = source[row, group, core if part == 0 else 1 - core]
                    for step in (-1, 0, 1):
                        at = (part * 3 + step + 1) * half + group * lanes
                        target[at : at + lanes, row * cols : (row + 1) * cols] = moved(
                            tile, step * dilation
                        )

    build(upper, taps_a)
    load.wait()
    copies = []
    for row_step, following in enumerate((own, lower, None)):
        result = jnp.dot(
            taps[row_step % 2][...], feats[...], preferred_element_type=jnp.float32
        )
        if following is not None:
            build(following, taps[(row_step + 1) % 2])
        slot = row_step % 2
        if row_step >= 2:
            for copy in copies[2 * (row_step - 2) : 2 * (row_step - 2) + 2]:
                copy.wait()
        sums[slot] = result
        for part, target in enumerate((keep_hbm, send_hbm)):
            copy = pltpu.make_async_copy(
                sums.at[slot, pl.ds(part * 3 * half, 3 * half)],
                target.at[row_step],
                out_sems.at[slot, part],
            )
            copy.start()
            copies.append(copy)
    for copy in copies[2:]:
        copy.wait()


def kernel_grad(core, upper, own, lower, feats, dilation):
    rows_dev, half_out, cols = own.shape
    chan = feats.shape[1]
    lanes = 16
    groups = half_out // (2 * lanes)
    split = lambda a: a.reshape(rows_dev, groups, 2, lanes, cols)
    vmem = pl.BlockSpec(memory_space=pltpu.VMEM)
    hbm = pl.BlockSpec(memory_space=pl.ANY)
    shape = jax.ShapeDtypeStruct((3, 3 * groups * lanes, chan), jnp.float32)
    keep, send = pl.pallas_call(
        functools.partial(kernel_grad_body, dilation),
        in_specs=[pl.BlockSpec(memory_space=pltpu.SMEM), vmem, vmem, vmem, hbm],
        out_specs=[hbm, hbm],
        out_shape=[shape, shape],
        scratch_shapes=[
            pltpu.VMEM(feats.shape, feats.dtype),
            pltpu.VMEM((3 * half_out, rows_dev * cols), own.dtype),
            pltpu.VMEM((3 * half_out, rows_dev * cols), own.dtype),
            pltpu.VMEM((2, 3 * half_out, chan), jnp.float32),
            pltpu.SemaphoreType.DMA,
            pltpu.SemaphoreType.DMA((2, 2)),
        ],
        compiler_params=pltpu.CompilerParams(vmem_limit_bytes=32 << 20),
        name="kernel_grad",
    )(core, split(upper), split(own), split(lower), feats)
    view = lambda a: a.reshape(9, groups, lanes, chan)
    return view(keep), view(send)


def input_grad_body(dilations, half_ref, *refs):
    count = len(dilations)
    tiles = refs[: 6 * count]
    weights_hbm, out, weights, taps, sem = refs[6 * count :]
    row = pl.program_id(0)
    cols = out.shape[1]
    half_out = tiles[0].shape[1]
    per_branch = 9 * 2 * half_out
    half = half_ref[0]
    loads = [
        pltpu.make_async_copy(weights_hbm.at[branch], weights.at[branch], sem.at[branch])
        for branch in range(count)
    ]

    @pl.when(row == 0)
    def _():
        for load in loads:
            load.start()

    total = None
    for branch, dilation in enumerate(dilations):
        for position in range(6):
            row_step, which = divmod(position, 2)
            tile = tiles[6 * branch + position][0]
            place = half if which == 0 else 1 - half
            for step in (-1, 0, 1):
                tap = row_step * 3 + step + 1
                at = pl.multiple_of(tap * 2 * half_out + place * half_out, half_out)
                taps[branch, pl.ds(at, half_out), :] = moved(tile, step * dilation)

        @pl.when(row == 0)
        def _():
            loads[branch].wait()

        part = jnp.dot(weights[branch], taps[branch], preferred_element_type=jnp.float32)
        total = part if total is None else total + part
    out[0] = total.astype(out.dtype).T


def input_grad(half, tiles, weights_t):
    rows_dev, half_out, cols = tiles[0].shape
    count, chan, depth = weights_t.shape
    spec = pl.BlockSpec((1, half_out, cols), lambda row, *_: (row, 0, 0))
    return pl.pallas_call(
        functools.partial(input_grad_body, RATES),
        grid_spec=pltpu.PrefetchScalarGridSpec(
            num_scalar_prefetch=1,
            grid=(rows_dev,),
            in_specs=[spec] * len(tiles) + [pl.BlockSpec(memory_space=pl.ANY)],
            out_specs=pl.BlockSpec((1, cols, chan), lambda row, *_: (row, 0, 0)),
            scratch_shapes=[
                pltpu.VMEM(weights_t.shape, weights_t.dtype),
                pltpu.VMEM((count, depth, cols), jnp.bfloat16),
                pltpu.SemaphoreType.DMA((count,)),
            ],
        ),
        out_shape=jax.ShapeDtypeStruct((rows_dev, cols, chan), jnp.bfloat16),
        compiler_params=pltpu.CompilerParams(vmem_limit_bytes=40 << 20),
        name="input_grad",
    )(half, *tiles, weights_t)


def partial_bound(features, masked):
    wide = features.astype(jnp.float32)
    feat_power = jnp.max(jnp.sum(wide * wide, axis=(0, 1)))
    wide = masked.astype(jnp.float32)
    mask_power = jnp.max(jnp.sum(wide * wide, axis=(1, 3)))
    both = jnp.where(lax.broadcasted_iota(jnp.int32, (8, 128), 0) < 4, feat_power, mask_power)
    bit = 1
    while bit < lax.axis_size("rows"):
        both = both + swapped(both, "rows", bit)
        bit *= 2
    other = swapped(both, "chan", 1)
    power = both[0, 0] * jnp.maximum(both[4, 0], other[4, 0])
    return jnp.maximum(jnp.sqrt(power) * 1.01, 1e-30)


def halved(total, axis, bit, position, grow, shrink):
    send = lax.dynamic_index_in_dim(total, 1 - position, axis, keepdims=False)
    keep = lax.dynamic_index_in_dim(total, position, axis, keepdims=False)
    got = swapped((send * grow).astype(jnp.float16), "rows", bit)
    return keep + got.astype(jnp.float32) * shrink


def shards(features, grad_out, pre_act, weights):
    rows_dev, cols, local_chan = features.shape
    out_chan = weights.shape[2]
    strips = lax.axis_size("rows")
    place = lax.axis_index("rows")
    half = lax.axis_index("chan")
    core, y_at, z_low, z_high = place % 2, place // 2 % 2, place // 4 % 2, place // 8
    masked = jnp.where(pre_act > 0, grad_out, jnp.zeros_like(grad_out))
    feats = features.reshape(rows_dev * cols, local_chan)

    own = [masked[branch] for branch in range(3)]
    upper = [fetch(own[branch], 1, dilation) for branch, dilation in enumerate(RATES)]
    lower = [fetch(own[branch], -1, dilation) for branch, dilation in enumerate(RATES)]
    other_masked = swapped(masked, "chan", 1)
    other_own = [other_masked[branch] for branch in range(3)]
    other_upper, other_lower = [], []
    for branch, dilation in enumerate(RATES):
        if branch in SHARED:
            pair = swapped(jnp.stack([upper[branch], lower[branch]]), "chan", 1)
            other_upper.append(pair[0])
            other_lower.append(pair[1])
        else:
            other_upper.append(fetch(other_own[branch], 1, dilation))
            other_lower.append(fetch(other_own[branch], -1, dilation))

    bound = partial_bound(features, masked)
    grow, shrink = 32000.0 / bound, bound / 32000.0
    weights_t = jnp.transpose(weights.reshape(3, 9 * out_chan, local_chan), (0, 2, 1))

    core_arg = core.astype(jnp.int32).reshape(1)
    across = [[], []]
    for share, sources in enumerate(((upper, own, lower), (other_upper, other_own, other_lower))):
        for branch, dilation in enumerate(RATES):
            keep, send = kernel_grad(core_arg, *(rows[branch] for rows in sources), feats, dilation)
            total = keep + swapped(send, "rows", 1)
            total = total.reshape(9, 2, 2, out_chan // strips, local_chan)
            if share == 0:
                total = halved(total, 2, 2, y_at, grow, shrink)
                total = halved(total, 1, 4, z_low, grow, shrink)
            else:
                total = halved(total, 1, 4, z_low, grow, shrink)
                total = halved(total, 1, 2, y_at, grow, shrink)
            pairs = []
            for row in range(strips):
                for chan in range(2):
                    target = chan if share == 0 else 1 - chan
                    if row // 8 != target:
                        pairs.append((row * 2 + chan, (row ^ 8) * 2 + chan))
            got = lax.ppermute((total * grow).astype(jnp.float16), ("rows", "chan"), pairs)
            across[share].append(total + got.astype(jnp.float32) * shrink)
    mine = z_high == half
    grad_weight = jnp.stack(
        [jnp.where(mine, across[0][branch], across[1][branch]) for branch in range(3)]
    )
    tiles = []
    for branch in range(3):
        for pair in ((upper, other_upper), (own, other_own), (lower, other_lower)):
            tiles += [pair[0][branch], pair[1][branch]]
    grad_input = input_grad(half.astype(jnp.int32).reshape(1), tiles, weights_t)
    return grad_input, grad_weight * grad_scale


def general(features, grad_out, pre_act, weights):
    rows_dev, cols, local_chan = features.shape
    out_chan = weights.shape[2]
    masked = grad_out * (pre_act > 0).astype(jnp.bfloat16)
    own_rows = lax.all_gather(masked, "chan", axis=2, tiled=True)
    kernels = weights.reshape(3, 9 * out_chan, local_chan)
    grad_input = jnp.zeros((rows_dev, cols, local_chan), jnp.float32)
    kernel_list = []
    for branch, dilation in enumerate(RATES):
        tap_list = []
        for row_step in (-1, 0, 1):
            rows = own_rows[branch]
            if row_step:
                rows = fetch(rows, -row_step, dilation)
            padded = jnp.pad(rows, ((0, 0), (0, 0), (dilation, dilation)))
            for col_step in (-1, 0, 1):
                cols_at = dilation - col_step * dilation
                tap_list.append(padded[:, :, cols_at : cols_at + cols])
        stacked_taps = jnp.concatenate(tap_list, axis=1)
        grad_input = grad_input + jnp.einsum(
            "rkc,ki->rci", stacked_taps, kernels[branch], preferred_element_type=jnp.float32
        )
        kernel_list.append(
            jnp.einsum("rkc,rci->ki", stacked_taps, features, preferred_element_type=jnp.float32)
        )
    partial_grad = jnp.stack(kernel_list, axis=0).reshape(3, 9, out_chan, local_chan)
    summed = lax.psum_scatter(partial_grad, "rows", scatter_dimension=2, tiled=True)
    return (grad_input.astype(jnp.bfloat16), summed * grad_scale)


def solution(mesh):
    in_specs = (
        P("rows", None, "chan"),
        P(None, "rows", "chan", None),
        P(None, "rows", "chan", None),
        P(None, None, None, "chan"),
    )
    out_specs = (P("rows", None, "chan"), P(None, None, "rows", "chan"))
    fast = mesh.shape["rows"] == 16 and mesh.shape["chan"] == 2
    body = shards if fast else general
    return jax.shard_map(body, mesh=mesh, in_specs=in_specs, out_specs=out_specs, check_vma=False)
```

```python
import functools

import jax
import jax.numpy as jnp
from jax import lax
from jax.experimental import pallas as pl
from jax.experimental.pallas import tpu as pltpu
from jax.sharding import PartitionSpec as P

RATES = (12, 24, 36)
grad_scale = 0.00390625
TOGETHER = 2
GRAD_PARTS = (4, 2, 2)


def passed_along(array, axis, by):
    count = lax.axis_size(axis)
    pairs = [(i, i + by) for i in range(count) if 0 <= i + by < count]
    return lax.ppermute(array, axis, pairs)


def swapped(array, axis, bit):
    count = lax.axis_size(axis)
    return lax.ppermute(array, axis, [(i, i ^ bit) for i in range(count)])


def row_pieces(dilation, side, rows_dev):
    start_strip = side * dilation // rows_dev
    remainder = side * dilation % rows_dev
    if remainder == 0:
        return [(start_strip, 0, rows_dev)]
    return [(start_strip, remainder, rows_dev), (start_strip + 1, 0, remainder)]


def fetch(source, side, dilation):
    return [
        passed_along(source[low:high], "rows", -strip)
        for strip, low, high in row_pieces(dilation, side, source.shape[0])
    ]


def after(values, gate):
    return lax.optimization_barrier((values, gate))[0]


def moved(tile, shift, axis):
    if shift == 0:
        return tile
    size = tile.shape[axis]
    at = lax.broadcasted_iota(jnp.int32, tile.shape, axis)
    keep = at >= shift if shift > 0 else at < size + shift
    return jnp.where(keep, pltpu.roll(tile, shift % size, axis), jnp.zeros_like(tile))


def kernel_grad_body(branch, dilation, y_first, bits_ref, own, pair, own_far, pair_far, feats_hbm,
                     feats_far_hbm, keep_out, send_out, feats, taps_near, taps_far, sums, sems):
    _, rows_dev, low, _, _, lanes, cols = own.shape
    core, first = bits_ref[0], bits_ref[1 if y_first else 2]
    loads = [
        pltpu.make_async_copy(source, feats.at[at], sems.at[at])
        for at, source in enumerate((feats_hbm, feats_far_hbm))
    ]
    for load in loads:
        load.start()

    def build(own_ref, pair_ref, turn, target):
        for row in range(TOGETHER):
            at_row = turn * TOGETHER + row
            for part in range(2):
                bit = first if part == 0 else 1 - first
                for row_step in range(3):
                    for group in range(low):
                        place = (group, bit, core) if y_first else (bit, group, core)
                        if row_step == 1:
                            tile = own_ref[(branch, at_row) + place]
                        else:
                            tile = pair_ref[(row_step // 2, at_row) + place]
                        for step in (-1, 0, 1):
                            tap = row_step * 3 + step + 1
                            at = ((part * low + group) * 9 + tap) * lanes
                            target[at : at + lanes, row * cols : (row + 1) * cols] = moved(
                                tile, step * dilation, 1
                            )

    build(own, pair, 0, taps_near)
    sums[...] = jnp.zeros_like(sums)
    turns = rows_dev // TOGETHER
    for load in loads:
        load.wait()

    def step(turn, carry):
        rows = pl.ds(pl.multiple_of(turn * TOGETHER * cols, TOGETHER * cols), TOGETHER * cols)
        sums[...] += jnp.dot(
            taps_near[...], feats[0, rows, :], preferred_element_type=jnp.float32
        )
        build(own_far, pair_far, turn, taps_far)
        sums[...] += jnp.dot(taps_far[...], feats[1, rows, :], preferred_element_type=jnp.float32)
        build(own, pair, jnp.minimum(turn + 1, turns - 1), taps_near)
        return carry

    lax.fori_loop(0, turns, step, 0)
    size = keep_out.shape[0]
    keep_out[...] = sums[:size]
    send_out[...] = sums[size:]


def kernel_grad(bits, near, far, feats, feats_far, branch, y_first, lanes):
    own, pair = near
    rows_dev, half_out, cols = own.shape[1:]
    chan = feats.shape[1]
    split = lambda a: a.reshape(a.shape[0], rows_dev, 2, 2, 2, lanes, cols)
    vmem = pl.BlockSpec(memory_space=pltpu.VMEM)
    hbm = pl.BlockSpec(memory_space=pl.ANY)
    depth = 9 * half_out // 2
    shape = jax.ShapeDtypeStruct((depth // 2, chan), jnp.float32)
    keep, send = pl.pallas_call(
        functools.partial(kernel_grad_body, branch, RATES[branch], y_first),
        in_specs=[pl.BlockSpec(memory_space=pltpu.SMEM)] + [vmem] * 4 + [hbm] * 2,
        out_specs=[vmem, vmem],
        out_shape=[shape, shape],
        scratch_shapes=[
            pltpu.VMEM((2,) + feats.shape, feats.dtype),
            pltpu.VMEM((depth, TOGETHER * cols), own.dtype),
            pltpu.VMEM((depth, TOGETHER * cols), own.dtype),
            pltpu.VMEM((depth, chan), jnp.float32),
            pltpu.SemaphoreType.DMA((2,)),
        ],
        compiler_params=pltpu.CompilerParams(vmem_limit_bytes=24 << 20),
        cost_estimate=pl.CostEstimate(
            flops=4 * depth * rows_dev * cols * chan,
            transcendentals=0,
            bytes_accessed=4 * feats.size + 4 * depth * chan,
        ),
        name="kernel_grad",
    )(bits, split(own), split(pair), split(far[0]), split(far[1]), feats, feats_far)
    view = lambda a: a.reshape(2, 9, lanes, chan)
    return view(keep), view(send)


def input_grad_body(together, first_row, half_ref, own, own_other, *refs):
    pairs, weights_hbm, (out, weights, taps, sems) = refs[:6], refs[6], refs[-4:]
    turn = pl.program_id(0)
    turns = pl.num_programs(0)
    half_out, cols = own.shape[2:]
    half = half_ref[0]
    count = weights.shape[0]
    loads = [
        pltpu.make_async_copy(weights_hbm.at[branch], weights.at[branch], sems.at[branch])
        for branch in range(count)
    ]

    def build(branch, at_turn):
        for row in range(together):
            at_row = first_row + at_turn * together + row
            for which in range(2):
                place = half if which == 0 else 1 - half
                for row_step in range(3):
                    if row_step == 1:
                        tile = (own, own_other)[which][branch, at_row]
                    else:
                        tile = pairs[2 * branch + which][row_step // 2, at_row]
                    turned = tile.T
                    for step in (-1, 0, 1):
                        tap = row_step * 3 + step + 1
                        at = pl.multiple_of((tap * 2 + place) * half_out, half_out)
                        taps[branch, row * cols : (row + 1) * cols, pl.ds(at, half_out)] = moved(
                            turned, step * RATES[branch], 0
                        )

    @pl.when(turn == 0)
    def _():
        for load in loads:
            load.start()
        build(0, 0)

    total = None
    for branch in range(count):

        @pl.when(turn == 0)
        def _():
            loads[branch].wait()

        part = jnp.dot(taps[branch], weights[branch], preferred_element_type=jnp.float32)
        total = part if total is None else total + part
        if branch + 1 < count:
            build(branch + 1, turn)
        else:
            build(0, jnp.minimum(turn + 1, turns - 1))
    out[...] = total.astype(out.dtype)


def input_grad(half, own, own_other, pairs, weights, first_row, rows, before, together=1):
    rows_dev, half_out, cols = own.shape[1:]
    count, depth, chan = weights.shape
    vmem = pl.BlockSpec(memory_space=pltpu.VMEM)
    operands = (half, own, own_other, *pairs, weights) + before
    return pl.pallas_call(
        functools.partial(input_grad_body, together, first_row),
        grid=(rows // together,),
        in_specs=[pl.BlockSpec(memory_space=pltpu.SMEM)]
        + [vmem] * 8
        + [pl.BlockSpec(memory_space=pl.ANY)] * (1 + len(before)),
        out_specs=pl.BlockSpec(
            (together * cols, chan), lambda turn: (turn + first_row // together, 0)
        ),
        input_output_aliases={10: 0} if before else {},
        scratch_shapes=[
            pltpu.VMEM(weights.shape, weights.dtype),
            pltpu.VMEM((count, together * cols, depth), own.dtype),
            pltpu.SemaphoreType.DMA((count,)),
        ],
        out_shape=jax.ShapeDtypeStruct((rows_dev * cols, chan), jnp.bfloat16),
        compiler_params=pltpu.CompilerParams(vmem_limit_bytes=36 << 20),
        cost_estimate=pl.CostEstimate(
            flops=2 * rows * cols * count * depth * chan,
            transcendentals=0,
            bytes_accessed=2 * weights.size + 2 * rows * cols * chan,
        ),
        name="input_grad",
    )(*operands)


def partial_bound(features, masked):
    wide = features.astype(jnp.float32)
    feat_power = jnp.max(jnp.sum(wide * wide, axis=(0, 1)))
    wide = masked.astype(jnp.float32)
    mask_power = jnp.max(jnp.sum(wide * wide, axis=(1, 3)))
    upper = lax.broadcasted_iota(jnp.int32, (8, 128), 0) < 4
    both = jnp.where(upper, feat_power, mask_power)
    other = swapped(both, "chan", 1)
    both = jnp.where(upper, both, jnp.maximum(both, other))
    bit = 1
    while bit < lax.axis_size("rows"):
        both = both + swapped(both, "rows", bit)
        bit *= 2
    return jnp.maximum(jnp.sqrt(both[0, 0]) * jnp.sqrt(both[4, 0]) * 1.01, 1e-30)


def shards(features, grad_out, pre_act, weights):
    rows_dev, cols, local_chan = features.shape
    out_chan = weights.shape[2]
    strips = lax.axis_size("rows")
    lanes = out_chan // strips
    place = lax.axis_index("rows")
    half = lax.axis_index("chan")
    core, y_at, z_low, z_high = place % 2, place // 2 % 2, place // 4 % 2, place // 8
    bits = jnp.stack([core, y_at, z_low]).astype(jnp.int32)
    half_arg = half.astype(jnp.int32).reshape(1)
    kernels = weights.reshape(3, 9 * out_chan, local_chan)
    masked = jnp.where(pre_act > 0, grad_out, jnp.zeros_like(grad_out))
    feats = features.reshape(rows_dev * cols, local_chan)
    feats_far = swapped(feats, "rows", 1)
    bound = partial_bound(features, masked)
    grow, shrink = 32000.0 / bound, bound / 32000.0

    own = [masked, swapped(masked, "chan", 1)]
    pairs = [
        [
            jnp.concatenate(
                fetch(masked[branch], 1, dilation) + fetch(masked[branch], -1, dilation)
            ).reshape((2,) + masked.shape[1:])
            for branch, dilation in enumerate(RATES)
        ]
    ]
    pairs.append([swapped(pair, "chan", 1) for pair in pairs[0]])
    own_far = [swapped(own[0], "rows", 1), None]
    pairs_far = [[swapped(pair, "rows", 1) for pair in pairs[0]], [None] * 3]

    def share_with_core(branch, gate):
        if branch == 0:
            own_far[1] = swapped(after(own[1], gate), "rows", 1)
        pairs_far[1][branch] = swapped(after(pairs[1][branch], gate), "rows", 1)


    def pack(values):
        return (values * grow).astype(jnp.float16)

    def unpack(values):
        return values.astype(jnp.float32) * shrink

    steps = [(share, branch) for share in range(2) for branch in range(3)]
    state, result = {}, {}

    def first_stage(at, gate):
        share, branch = steps[at]
        keep, send = kernel_grad(
            after(bits, gate),
            (own[share], pairs[share][branch]),
            (own_far[share], pairs_far[share][branch]),
            feats,
            feats_far,
            branch,
            share == 0,
            lanes,
        )
        send = pack(send)
        state[at] = (keep, swapped(send, "rows", 2 if share == 0 else 4))
        return [send, keep]

    def second_stage(at):
        share = steps[at][0]
        keep, got = state[at]
        total = keep + unpack(got)
        position, bit = (z_low, 4) if share == 0 else (y_at, 2)
        send = pack(lax.dynamic_index_in_dim(total, 1 - position, 0, keepdims=False))
        keep = lax.dynamic_index_in_dim(total, position, 0, keepdims=False)
        state[at] = (keep, swapped(send, "rows", bit))
        return [send, keep]

    def third_stage(at):
        share = steps[at][0]
        keep, got = state[at]
        total = keep + unpack(got)
        pairs = [
            (row * 2 + chan, (row ^ 8) * 2 + chan)
            for row in range(strips)
            for chan in range(2)
            if row // 8 != (chan if share == 0 else 1 - chan)
        ]
        send = pack(total)
        state[at] = (total, lax.ppermute(send, ("rows", "chan"), pairs))
        return [send, total]

    def last_stage(at):
        keep, got = state[at]
        result[at] = keep + unpack(got)
        return [result[at]]

    row_parts = []
    first_row = 0

    def rows_of_input_grad(count, gate):
        nonlocal first_row
        flat = [pairs[share][branch] for branch in range(3) for share in range(2)]
        row_parts.append(
            input_grad(
                after(half_arg, gate),
                own[0],
                own[1],
                flat,
                kernels,
                first_row,
                count,
                tuple(row_parts[-1:]),
            )
        )
        first_row += count
        return [row_parts[-1]]

    gate = []
    gate = first_stage(0, gate)
    gate = first_stage(1, gate)
    share_with_core(0, gate)
    gate = first_stage(2, gate)
    gate += second_stage(0)
    gate = first_stage(3, gate)
    share_with_core(1, gate)
    gate += second_stage(1) + third_stage(0)
    gate = first_stage(4, gate)
    share_with_core(2, gate)
    gate += second_stage(2) + third_stage(1)
    gate = first_stage(5, gate)
    gate += second_stage(3) + third_stage(2)
    gate = rows_of_input_grad(GRAD_PARTS[0], gate)
    gate += second_stage(4) + third_stage(3)
    gate += second_stage(5)
    gate = rows_of_input_grad(GRAD_PARTS[1], gate)
    gate += third_stage(4) + third_stage(5)
    rows_of_input_grad(GRAD_PARTS[2], gate)
    for at in range(6):
        last_stage(at)
    mine = z_high == half
    grad_weight = jnp.stack(
        [jnp.where(mine, result[branch], result[3 + branch]) for branch in range(3)]
    )
    grad_input = row_parts[-1].reshape(rows_dev, cols, local_chan)
    return grad_input, grad_weight * grad_scale


def general(features, grad_out, pre_act, weights):
    rows_dev, cols, local_chan = features.shape
    out_chan = weights.shape[2]
    masked = grad_out * (pre_act > 0).astype(jnp.bfloat16)
    own_rows = lax.all_gather(masked, "chan", axis=2, tiled=True)
    kernels = weights.reshape(3, 9 * out_chan, local_chan)
    grad_input = jnp.zeros((rows_dev, cols, local_chan), jnp.float32)
    kernel_list = []
    for branch, dilation in enumerate(RATES):
        tap_list = []
        for row_step in (-1, 0, 1):
            rows = own_rows[branch]
            if row_step:
                rows = jnp.concatenate(fetch(rows, -row_step, dilation))
            padded = jnp.pad(rows, ((0, 0), (0, 0), (dilation, dilation)))
            for col_step in (-1, 0, 1):
                cols_at = dilation - col_step * dilation
                tap_list.append(padded[:, :, cols_at : cols_at + cols])
        stacked_taps = jnp.concatenate(tap_list, axis=1)
        grad_input = grad_input + jnp.einsum(
            "rkc,ki->rci", stacked_taps, kernels[branch], preferred_element_type=jnp.float32
        )
        kernel_list.append(
            jnp.einsum("rkc,rci->ki", stacked_taps, features, preferred_element_type=jnp.float32)
        )
    partial_grad = jnp.stack(kernel_list, axis=0).reshape(3, 9, out_chan, local_chan)
    summed = lax.psum_scatter(partial_grad, "rows", scatter_dimension=2, tiled=True)
    return (grad_input.astype(jnp.bfloat16), summed * grad_scale)


def solution(mesh):
    in_specs = (
        P("rows", None, "chan"),
        P(None, "rows", "chan", None),
        P(None, "rows", "chan", None),
        P(None, None, None, "chan"),
    )
    out_specs = (P("rows", None, "chan"), P(None, None, "rows", "chan"))
    fast = mesh.shape["rows"] == 16 and mesh.shape["chan"] == 2
    body = shards if fast else general
    return jax.shard_map(body, mesh=mesh, in_specs=in_specs, out_specs=out_specs, check_vma=False)
```

```python
import functools

import jax
import jax.numpy as jnp
from jax import lax
from jax.experimental import pallas as pl
from jax.experimental.pallas import tpu as pltpu
from jax.sharding import PartitionSpec as P

RATES = (12, 24, 36)
grad_scale = 0.00390625
TOGETHER = 2
GRAD_PARTS = (4, 2, 2)


def passed_along(array, axis, by):
    count = lax.axis_size(axis)
    pairs = [(i, i + by) for i in range(count) if 0 <= i + by < count]
    return lax.ppermute(array, axis, pairs)


def swapped(array, axis, bit):
    count = lax.axis_size(axis)
    return lax.ppermute(array, axis, [(i, i ^ bit) for i in range(count)])


def row_pieces(dilation, side, rows_dev):
    start_strip = side * dilation // rows_dev
    remainder = side * dilation % rows_dev
    if remainder == 0:
        return [(start_strip, 0, rows_dev)]
    return [(start_strip, remainder, rows_dev), (start_strip + 1, 0, remainder)]


def fetch(source, side, dilation):
    return [
        passed_along(source[low:high], "rows", -strip)
        for strip, low, high in row_pieces(dilation, side, source.shape[0])
    ]


def after(values, gate):
    return lax.optimization_barrier((values, gate))[0]


def moved(tile, shift, axis):
    if shift == 0:
        return tile
    size = tile.shape[axis]
    at = lax.broadcasted_iota(jnp.int32, tile.shape, axis)
    keep = at >= shift if shift > 0 else at < size + shift
    return jnp.where(keep, pltpu.roll(tile, shift % size, axis), jnp.zeros_like(tile))


def joined_body(*refs):
    at = 0
    for piece in refs[:-1]:
        refs[-1][at : at + piece.shape[0]] = piece[...]
        at += piece.shape[0]


def joined(pieces):
    count = sum(piece.shape[0] for piece in pieces)
    vmem = pl.BlockSpec(memory_space=pltpu.VMEM)
    return pl.pallas_call(
        joined_body,
        in_specs=[vmem] * len(pieces),
        out_specs=vmem,
        out_shape=jax.ShapeDtypeStruct((count,) + pieces[0].shape[1:], pieces[0].dtype),
        name="joined",
    )(*pieces)


def kernel_grad_body(branch, dilation, y_first, bits_ref, own, pair, own_far, pair_far, feats,
                     feats_far, keep_out, send_out, taps_near, taps_far, sums):
    _, rows_dev, low, _, _, lanes, cols = own.shape
    core, first = bits_ref[0], bits_ref[1 if y_first else 2]

    def build(own_ref, pair_ref, turn, target):
        for row in range(TOGETHER):
            at_row = turn * TOGETHER + row
            for part in range(2):
                bit = first if part == 0 else 1 - first
                for row_step in range(3):
                    for group in range(low):
                        place = (group, bit, core) if y_first else (bit, group, core)
                        if row_step == 1:
                            tile = own_ref[(branch, at_row) + place]
                        else:
                            tile = pair_ref[(row_step // 2, at_row) + place]
                        for step in (-1, 0, 1):
                            tap = row_step * 3 + step + 1
                            at = ((part * low + group) * 9 + tap) * lanes
                            target[at : at + lanes, row * cols : (row + 1) * cols] = moved(
                                tile, step * dilation, 1
                            )

    build(own, pair, 0, taps_near)
    sums[...] = jnp.zeros_like(sums)
    turns = rows_dev // TOGETHER

    def step(turn, carry):
        rows = pl.ds(pl.multiple_of(turn * TOGETHER * cols, TOGETHER * cols), TOGETHER * cols)
        sums[...] += jnp.dot(
            taps_near[...], feats[rows, :], preferred_element_type=jnp.float32
        )
        build(own_far, pair_far, turn, taps_far)
        sums[...] += jnp.dot(taps_far[...], feats_far[rows, :], preferred_element_type=jnp.float32)
        build(own, pair, jnp.minimum(turn + 1, turns - 1), taps_near)
        return carry

    lax.fori_loop(0, turns, step, 0)
    size = keep_out.shape[0]
    keep_out[...] = sums[:size]
    send_out[...] = sums[size:]


def kernel_grad(bits, near, far, feats, feats_far, branch, y_first, lanes):
    own, pair = near
    rows_dev, half_out, cols = own.shape[1:]
    chan = feats.shape[1]
    split = lambda a: a.reshape(a.shape[0], rows_dev, 2, 2, 2, lanes, cols)
    vmem = pl.BlockSpec(memory_space=pltpu.VMEM)
    depth = 9 * half_out // 2
    shape = jax.ShapeDtypeStruct((depth // 2, chan), jnp.float32)
    keep, send = pl.pallas_call(
        functools.partial(kernel_grad_body, branch, RATES[branch], y_first),
        in_specs=[pl.BlockSpec(memory_space=pltpu.SMEM)] + [vmem] * 6,
        out_specs=[vmem, vmem],
        out_shape=[shape, shape],
        scratch_shapes=[
            pltpu.VMEM((depth, TOGETHER * cols), own.dtype),
            pltpu.VMEM((depth, TOGETHER * cols), own.dtype),
            pltpu.VMEM((depth, chan), jnp.float32),
        ],
        compiler_params=pltpu.CompilerParams(vmem_limit_bytes=20 << 20),
        cost_estimate=pl.CostEstimate(
            flops=4 * depth * rows_dev * cols * chan,
            transcendentals=0,
            bytes_accessed=4 * feats.size + 4 * depth * chan,
        ),
        name="kernel_grad",
    )(bits, split(own), split(pair), split(far[0]), split(far[1]), feats, feats_far)
    view = lambda a: a.reshape(2, 9, lanes, chan)
    return view(keep), view(send)


def input_grad_body(together, first_row, half_ref, own, own_other, *refs):
    pairs, weights, (out, taps) = refs[:6], refs[6], refs[-2:]
    turn = pl.program_id(0)
    turns = pl.num_programs(0)
    half_out, cols = own.shape[2:]
    half = half_ref[0]
    count = weights.shape[0]

    def build(branch, at_turn):
        for row in range(together):
            at_row = first_row + at_turn * together + row
            for which in range(2):
                place = half if which == 0 else 1 - half
                for row_step in range(3):
                    if row_step == 1:
                        tile = (own, own_other)[which][branch, at_row]
                    else:
                        tile = pairs[2 * branch + which][row_step // 2, at_row]
                    turned = tile.T
                    for step in (-1, 0, 1):
                        tap = row_step * 3 + step + 1
                        at = pl.multiple_of((tap * 2 + place) * half_out, half_out)
                        taps[branch, row * cols : (row + 1) * cols, pl.ds(at, half_out)] = moved(
                            turned, step * RATES[branch], 0
                        )

    @pl.when(turn == 0)
    def _():
        build(0, 0)

    total = None
    for branch in range(count):
        part = jnp.dot(taps[branch], weights[branch], preferred_element_type=jnp.float32)
        total = part if total is None else total + part
        if branch + 1 < count:
            build(branch + 1, turn)
        else:
            build(0, jnp.minimum(turn + 1, turns - 1))
    out[...] = total.astype(out.dtype)


def input_grad(half, own, own_other, pairs, weights, first_row, rows, before, together=1):
    rows_dev, _, cols = own.shape[1:]
    count, depth, chan = weights.shape
    vmem = pl.BlockSpec(memory_space=pltpu.VMEM)
    operands = (half, own, own_other, *pairs, weights) + before
    return pl.pallas_call(
        functools.partial(input_grad_body, together, first_row),
        grid=(rows // together,),
        in_specs=[pl.BlockSpec(memory_space=pltpu.SMEM)]
        + [vmem] * 9
        + [pl.BlockSpec(memory_space=pl.ANY)] * len(before),
        out_specs=pl.BlockSpec(
            (together * cols, chan), lambda turn: (turn + first_row // together, 0)
        ),
        input_output_aliases={10: 0} if before else {},
        scratch_shapes=[
            pltpu.VMEM((count, together * cols, depth), own.dtype),
        ],
        out_shape=jax.ShapeDtypeStruct((rows_dev * cols, chan), jnp.bfloat16),
        compiler_params=pltpu.CompilerParams(vmem_limit_bytes=20 << 20),
        cost_estimate=pl.CostEstimate(
            flops=2 * rows * cols * count * depth * chan,
            transcendentals=0,
            bytes_accessed=2 * weights.size + 2 * rows * cols * chan,
        ),
        name="input_grad",
    )(*operands)


def partial_bound(features, masked):
    wide = features.astype(jnp.float32)
    feat_power = jnp.max(jnp.sum(wide * wide, axis=(0, 1)))
    wide = masked.astype(jnp.float32)
    mask_power = jnp.max(jnp.sum(wide * wide, axis=(1, 3)))
    upper = lax.broadcasted_iota(jnp.int32, (8, 128), 0) < 4
    both = jnp.where(upper, feat_power, mask_power)
    other = swapped(both, "chan", 1)
    both = jnp.where(upper, both, jnp.maximum(both, other))
    bit = 1
    while bit < lax.axis_size("rows"):
        both = both + swapped(both, "rows", bit)
        bit *= 2
    return jnp.maximum(jnp.sqrt(both[0, 0]) * jnp.sqrt(both[4, 0]) * 1.01, 1e-30)


def shards(features, grad_out, pre_act, weights):
    rows_dev, cols, local_chan = features.shape
    out_chan = weights.shape[2]
    strips = lax.axis_size("rows")
    lanes = out_chan // strips
    place = lax.axis_index("rows")
    half = lax.axis_index("chan")
    core, y_at, z_low, z_high = place % 2, place // 2 % 2, place // 4 % 2, place // 8
    bits = jnp.stack([core, y_at, z_low]).astype(jnp.int32)
    half_arg = half.astype(jnp.int32).reshape(1)
    kernels = weights.reshape(3, 9 * out_chan, local_chan)
    masked = jnp.where(pre_act > 0, grad_out, jnp.zeros_like(grad_out))
    feats = features.reshape(rows_dev * cols, local_chan)
    feats_far = swapped(feats, "rows", 1)
    bound = partial_bound(features, masked)
    grow, shrink = 32000.0 / bound, bound / 32000.0

    own = [masked, swapped(masked, "chan", 1)]
    pairs = [[], []]
    for branch, dilation in enumerate(RATES):
        pieces = fetch(masked[branch], 1, dilation) + fetch(masked[branch], -1, dilation)
        pairs[0].append(joined(pieces).reshape((2,) + masked.shape[1:]))
        pairs[1].append(swapped(pairs[0][branch], "chan", 1))
    own_far = [swapped(own[0], "rows", 1), None]
    pairs_far = [[swapped(pair, "rows", 1) for pair in pairs[0]], [None] * 3]

    def share_with_core(branch, gate):
        if branch == 0:
            own_far[1] = swapped(after(own[1], gate), "rows", 1)
        pairs_far[1][branch] = swapped(after(pairs[1][branch], gate), "rows", 1)


    def pack(values):
        return (values * grow).astype(jnp.float16)

    def unpack(values):
        return values.astype(jnp.float32) * shrink

    steps = [(share, branch) for share in range(2) for branch in range(3)]
    state, result = {}, {}

    def first_stage(at, gate):
        share, branch = steps[at]
        keep, send = kernel_grad(
            after(bits, gate),
            (own[share], pairs[share][branch]),
            (own_far[share], pairs_far[share][branch]),
            feats,
            feats_far,
            branch,
            share == 0,
            lanes,
        )
        send = pack(send)
        state[at] = (keep, swapped(send, "rows", 2 if share == 0 else 4))
        return [send, keep]

    def second_stage(at, gate):
        share = steps[at][0]
        keep, got = after(state[at], gate)
        total = keep + unpack(got)
        position, bit = (z_low, 4) if share == 0 else (y_at, 2)
        send = pack(lax.dynamic_index_in_dim(total, 1 - position, 0, keepdims=False))
        keep = lax.dynamic_index_in_dim(total, position, 0, keepdims=False)
        state[at] = (keep, swapped(send, "rows", bit))
        return [send, keep]

    def third_stage(at, gate):
        share = steps[at][0]
        keep, got = after(state[at], gate)
        total = keep + unpack(got)
        pairs = [
            (row * 2 + chan, (row ^ 8) * 2 + chan)
            for row in range(strips)
            for chan in range(2)
            if row // 8 != (chan if share == 0 else 1 - chan)
        ]
        send = pack(total)
        state[at] = (total, lax.ppermute(send, ("rows", "chan"), pairs))
        return [send, total]

    def last_stage(at, gate):
        keep, got = after(state[at], gate)
        result[at] = keep + unpack(got)
        return [result[at]]

    row_parts = []
    first_row = 0

    def rows_of_input_grad(count, gate):
        nonlocal first_row
        flat = [pairs[share][branch] for branch in range(3) for share in range(2)]
        row_parts.append(
            input_grad(
                after(half_arg, gate),
                own[0],
                own[1],
                flat,
                kernels,
                first_row,
                count,
                tuple(row_parts[-1:]),
            )
        )
        first_row += count
        return [row_parts[-1]]

    gate = first_stage(0, [])
    gate = first_stage(1, gate)
    share_with_core(0, gate)
    ready = gate = first_stage(2, gate)
    gate = ready + second_stage(0, ready)
    share_with_core(1, gate)
    ready = gate = first_stage(3, gate)
    gate = ready + second_stage(1, ready)
    share_with_core(2, gate)
    ready = gate = first_stage(4, gate)
    gate = ready + second_stage(2, ready) + third_stage(0, ready)
    ready = gate = first_stage(5, gate)
    gate = ready + second_stage(3, ready) + third_stage(1, ready)
    ready = rows_of_input_grad(GRAD_PARTS[0], gate)
    gate = ready + second_stage(4, ready) + second_stage(5, ready) + third_stage(2, ready)
    ready = rows_of_input_grad(GRAD_PARTS[1], gate)
    gate = ready + third_stage(3, ready) + third_stage(4, ready) + third_stage(5, ready)
    ready = rows_of_input_grad(GRAD_PARTS[2], gate)
    for at in range(6):
        last_stage(at, ready)
    mine = z_high == half
    grad_weight = jnp.stack(
        [jnp.where(mine, result[branch], result[3 + branch]) for branch in range(3)]
    )
    grad_input = row_parts[-1].reshape(rows_dev, cols, local_chan)
    return grad_input, grad_weight * grad_scale


def general(features, grad_out, pre_act, weights):
    rows_dev, cols, local_chan = features.shape
    out_chan = weights.shape[2]
    masked = grad_out * (pre_act > 0).astype(jnp.bfloat16)
    own_rows = lax.all_gather(masked, "chan", axis=2, tiled=True)
    kernels = weights.reshape(3, 9 * out_chan, local_chan)
    grad_input = jnp.zeros((rows_dev, cols, local_chan), jnp.float32)
    kernel_list = []
    for branch, dilation in enumerate(RATES):
        tap_list = []
        for row_step in (-1, 0, 1):
            rows = own_rows[branch]
            if row_step:
                rows = jnp.concatenate(fetch(rows, -row_step, dilation))
            padded = jnp.pad(rows, ((0, 0), (0, 0), (dilation, dilation)))
            for col_step in (-1, 0, 1):
                cols_at = dilation - col_step * dilation
                tap_list.append(padded[:, :, cols_at : cols_at + cols])
        stacked_taps = jnp.concatenate(tap_list, axis=1)
        grad_input = grad_input + jnp.einsum(
            "rkc,ki->rci", stacked_taps, kernels[branch], preferred_element_type=jnp.float32
        )
        kernel_list.append(
            jnp.einsum("rkc,rci->ki", stacked_taps, features, preferred_element_type=jnp.float32)
        )
    partial_grad = jnp.stack(kernel_list, axis=0).reshape(3, 9, out_chan, local_chan)
    summed = lax.psum_scatter(partial_grad, "rows", scatter_dimension=2, tiled=True)
    return (grad_input.astype(jnp.bfloat16), summed * grad_scale)


def solution(mesh):
    in_specs = (
        P("rows", None, "chan"),
        P(None, "rows", "chan", None),
        P(None, "rows", "chan", None),
        P(None, None, None, "chan"),
    )
    out_specs = (P("rows", None, "chan"), P(None, None, "rows", "chan"))
    fast = mesh.shape["rows"] == 16 and mesh.shape["chan"] == 2
    if not fast:
        return jax.shard_map(
            general, mesh=mesh, in_specs=in_specs, out_specs=out_specs, check_vma=False
        )

    return jax.shard_map(shards, mesh=mesh, in_specs=in_specs, out_specs=out_specs, check_vma=False)
```

```python
import functools

import jax
import jax.numpy as jnp
from jax import lax
from jax.experimental import pallas as pl
from jax.experimental.pallas import tpu as pltpu
from jax.sharding import PartitionSpec as P

RATES = (12, 24, 36)
grad_scale = 0.00390625
TOGETHER = 2
GRAD_PARTS = (4, 2, 2)


def passed_along(array, axis, by):
    count = lax.axis_size(axis)
    pairs = [(i, i + by) for i in range(count) if 0 <= i + by < count]
    return lax.ppermute(array, axis, pairs)


def swapped(array, axis, bit):
    count = lax.axis_size(axis)
    return lax.ppermute(array, axis, [(i, i ^ bit) for i in range(count)])


def row_pieces(dilation, side, rows_dev):
    start_strip = side * dilation // rows_dev
    remainder = side * dilation % rows_dev
    if remainder == 0:
        return [(start_strip, 0, rows_dev)]
    return [(start_strip, remainder, rows_dev), (start_strip + 1, 0, remainder)]


def fetch(source, side, dilation):
    return [
        passed_along(source[low:high], "rows", -strip)
        for strip, low, high in row_pieces(dilation, side, source.shape[0])
    ]


def after(values, gate):
    return lax.optimization_barrier((values, gate))[0]


def moved(tile, shift, axis):
    if shift == 0:
        return tile
    size = tile.shape[axis]
    at = lax.broadcasted_iota(jnp.int32, tile.shape, axis)
    keep = at >= shift if shift > 0 else at < size + shift
    return jnp.where(keep, pltpu.roll(tile, shift % size, axis), jnp.zeros_like(tile))


def joined(pieces):
    if len({piece.shape for piece in pieces}) == 1:
        stacked = jnp.stack(pieces)
        return stacked.reshape((-1,) + stacked.shape[2:])
    return jnp.concatenate(pieces)


def kernel_grad_body(branch, dilation, bits_ref, own, pair, own_far, pair_far, feats,
                     feats_far, keep_out, send_out, taps_near, taps_far, sums):
    _, rows_dev, low, _, _, lanes, cols = own.shape
    core, first = bits_ref[0], bits_ref[1]

    def build(own_ref, pair_ref, turn, target):
        for row in range(TOGETHER):
            at_row = turn * TOGETHER + row
            for part in range(2):
                bit = first if part == 0 else 1 - first
                for row_step in range(3):
                    for group in range(low):
                        place = (group, bit, core)
                        if row_step == 1:
                            tile = own_ref[(branch, at_row) + place]
                        else:
                            tile = pair_ref[(row_step // 2, at_row) + place]
                        for step in (-1, 0, 1):
                            tap = row_step * 3 + step + 1
                            at = ((part * low + group) * 9 + tap) * lanes
                            target[at : at + lanes, row * cols : (row + 1) * cols] = moved(
                                tile, step * dilation, 1
                            )

    build(own, pair, 0, taps_near)
    sums[...] = jnp.zeros_like(sums)
    turns = rows_dev // TOGETHER

    def step(turn, carry):
        rows = pl.ds(pl.multiple_of(turn * TOGETHER * cols, TOGETHER * cols), TOGETHER * cols)
        sums[...] += jnp.dot(
            taps_near[...], feats[rows, :], preferred_element_type=jnp.float32
        )
        build(own_far, pair_far, turn, taps_far)
        sums[...] += jnp.dot(taps_far[...], feats_far[rows, :], preferred_element_type=jnp.float32)
        build(own, pair, jnp.minimum(turn + 1, turns - 1), taps_near)
        return carry

    lax.fori_loop(0, turns, step, 0)
    size = keep_out.shape[0]
    keep_out[...] = sums[:size]
    send_out[...] = sums[size:]


def kernel_grad(bits, near, far, feats, feats_far, branch, lanes):
    own, pair = near
    rows_dev, half_out, cols = own.shape[1:]
    chan = feats.shape[1]
    split = lambda a: a.reshape(a.shape[0], rows_dev, 2, 2, 2, lanes, cols)
    vmem = pl.BlockSpec(memory_space=pltpu.VMEM)
    depth = 9 * half_out // 2
    shape = jax.ShapeDtypeStruct((depth // 2, chan), jnp.float32)
    keep, send = pl.pallas_call(
        functools.partial(kernel_grad_body, branch, RATES[branch]),
        in_specs=[pl.BlockSpec(memory_space=pltpu.SMEM)] + [vmem] * 6,
        out_specs=[vmem, vmem],
        out_shape=[shape, shape],
        scratch_shapes=[
            pltpu.VMEM((depth, TOGETHER * cols), own.dtype),
            pltpu.VMEM((depth, TOGETHER * cols), own.dtype),
            pltpu.VMEM((depth, chan), jnp.float32),
        ],
        compiler_params=pltpu.CompilerParams(vmem_limit_bytes=20 << 20),
        cost_estimate=pl.CostEstimate(
            flops=4 * depth * rows_dev * cols * chan,
            transcendentals=0,
            bytes_accessed=4 * feats.size + 4 * depth * chan,
        ),
        name="kernel_grad",
    )(bits, split(own), split(pair), split(far[0]), split(far[1]), feats, feats_far)
    view = lambda a: a.reshape(2, 9, lanes, chan)
    return view(keep), view(send)


def input_grad_body(together, first_row, half_ref, own, own_other, *refs):
    pairs, weights, (out, taps) = refs[:6], refs[6], refs[-2:]
    turn = pl.program_id(0)
    turns = pl.num_programs(0)
    half_out, cols = own.shape[2:]
    half = half_ref[0]
    count = weights.shape[0]

    def build(branch, at_turn):
        for row in range(together):
            at_row = first_row + at_turn * together + row
            for which in range(2):
                place = half if which == 0 else 1 - half
                for row_step in range(3):
                    if row_step == 1:
                        tile = (own, own_other)[which][branch, at_row]
                    else:
                        tile = pairs[2 * branch + which][row_step // 2, at_row]
                    turned = tile.T
                    for step in (-1, 0, 1):
                        tap = row_step * 3 + step + 1
                        at = pl.multiple_of((tap * 2 + place) * half_out, half_out)
                        taps[branch, row * cols : (row + 1) * cols, pl.ds(at, half_out)] = moved(
                            turned, step * RATES[branch], 0
                        )

    @pl.when(turn == 0)
    def _():
        build(0, 0)

    total = None
    for branch in range(count):
        part = jnp.dot(taps[branch], weights[branch], preferred_element_type=jnp.float32)
        total = part if total is None else total + part
        if branch + 1 < count:
            build(branch + 1, turn)
        else:
            build(0, jnp.minimum(turn + 1, turns - 1))
    out[...] = total.astype(out.dtype)


def input_grad(half, own, own_other, pairs, weights, first_row, rows, before, together=1):
    rows_dev, _, cols = own.shape[1:]
    count, depth, chan = weights.shape
    vmem = pl.BlockSpec(memory_space=pltpu.VMEM)
    operands = (half, own, own_other, *pairs, weights) + before
    return pl.pallas_call(
        functools.partial(input_grad_body, together, first_row),
        grid=(rows // together,),
        in_specs=[pl.BlockSpec(memory_space=pltpu.SMEM)]
        + [vmem] * 9
        + [pl.BlockSpec(memory_space=pl.ANY)] * len(before),
        out_specs=pl.BlockSpec(
            (together * cols, chan), lambda turn: (turn + first_row // together, 0)
        ),
        input_output_aliases={10: 0} if before else {},
        scratch_shapes=[
            pltpu.VMEM((count, together * cols, depth), own.dtype),
        ],
        out_shape=jax.ShapeDtypeStruct((rows_dev * cols, chan), jnp.bfloat16),
        compiler_params=pltpu.CompilerParams(vmem_limit_bytes=20 << 20),
        cost_estimate=pl.CostEstimate(
            flops=2 * rows * cols * count * depth * chan,
            transcendentals=0,
            bytes_accessed=2 * weights.size + 2 * rows * cols * chan,
        ),
        name="input_grad",
    )(*operands)


def partial_bound(features, masked):
    wide = masked.astype(jnp.float32)
    mask_power = jnp.broadcast_to(jnp.max(jnp.sum(wide * wide, axis=(1, 3))), (8, 128))
    mask_power = jnp.maximum(mask_power, swapped(mask_power, "chan", 1))
    wide = features.astype(jnp.float32)
    feat_power = jnp.max(jnp.sum(wide * wide, axis=(0, 1)))
    upper = lax.broadcasted_iota(jnp.int32, (8, 128), 0) < 4
    both = jnp.where(upper, feat_power, mask_power)
    bit = 1
    while bit < lax.axis_size("rows"):
        both = both + swapped(both, "rows", bit)
        bit *= 2
    return jnp.maximum(jnp.sqrt(both[0, 0]) * jnp.sqrt(both[4, 0]) * 1.01, 1e-30)


def shards(features, grad_out, pre_act, weights):
    rows_dev, cols, local_chan = features.shape
    out_chan = weights.shape[2]
    strips = lax.axis_size("rows")
    lanes = out_chan // strips
    place = lax.axis_index("rows")
    half = lax.axis_index("chan")
    core, y_at, z_low, z_high = place % 2, place // 2 % 2, place // 4 % 2, place // 8
    bits = jnp.stack([core, y_at]).astype(jnp.int32)
    half_arg = half.astype(jnp.int32).reshape(1)
    kernels = weights.reshape(3, 9 * out_chan, local_chan)
    masked = jnp.where(pre_act > 0, grad_out, jnp.zeros_like(grad_out))
    feats = features.reshape(rows_dev * cols, local_chan)
    feats_far = swapped(feats, "rows", 1)
    bound = partial_bound(features, masked)
    grow, shrink = 32000.0 / bound, bound / 32000.0

    own = [masked, swapped(masked, "chan", 1)]
    pieces = []
    for branch, dilation in enumerate(RATES):
        pieces.append(fetch(masked[branch], 1, dilation) + fetch(masked[branch], -1, dilation))
    own_far = [swapped(own[0], "rows", 1), None]
    pairs, pairs_far = [[None] * 3, [None] * 3], [[None] * 3, [None] * 3]

    def join(branch, gate):
        pair = joined(after(pieces[branch], gate)).reshape((2,) + masked.shape[1:])
        pairs[1][branch] = swapped(pair, "chan", 1)
        pairs[0][branch] = pair
        pairs_far[0][branch] = swapped(pair, "rows", 1)

    def share_with_core(branch, gate):
        if branch == 0:
            own_far[1] = swapped(after(own[1], gate), "rows", 1)
        pairs_far[1][branch] = swapped(after(pairs[1][branch], gate), "rows", 1)


    def pack(values):
        return (values * grow).astype(jnp.float16)

    def unpack(values):
        return values.astype(jnp.float32) * shrink

    steps = [(share, branch) for share in range(2) for branch in range(3)]
    state, result = {}, {}

    def first_stage(at, gate):
        share, branch = steps[at]
        keep, send = kernel_grad(
            after(bits, gate),
            (own[share], pairs[share][branch]),
            (own_far[share], pairs_far[share][branch]),
            feats,
            feats_far,
            branch,
            lanes,
        )
        send = pack(send)
        state[at] = (keep, swapped(send, "rows", 2))
        return [send, keep]

    def second_stage(at, gate):
        keep, got = after(state[at], gate)
        total = keep + unpack(got)
        send = pack(lax.dynamic_index_in_dim(total, 1 - z_low, 0, keepdims=False))
        keep = lax.dynamic_index_in_dim(total, z_low, 0, keepdims=False)
        state[at] = (keep, swapped(send, "rows", 4))
        return [send, keep]

    def third_stage(at, gate):
        share = steps[at][0]
        keep, got = after(state[at], gate)
        total = keep + unpack(got)
        pairs = [
            (row * 2 + chan, (row ^ 8) * 2 + chan)
            for row in range(strips)
            for chan in range(2)
            if row // 8 != (chan if share == 0 else 1 - chan)
        ]
        send = pack(total)
        state[at] = (total, lax.ppermute(send, ("rows", "chan"), pairs))
        return [send, total]

    def last_stage(at, gate):
        keep, got = after(state[at], gate)
        result[at] = keep + unpack(got)
        return [result[at]]

    row_parts = []
    first_row = 0

    def rows_of_input_grad(count, gate):
        nonlocal first_row
        flat = [pairs[share][branch] for branch in range(3) for share in range(2)]
        row_parts.append(
            input_grad(
                after(half_arg, gate),
                own[0],
                own[1],
                flat,
                kernels,
                first_row,
                count,
                tuple(row_parts[-1:]),
            )
        )
        first_row += count
        return [row_parts[-1]]

    join(0, [])
    join(1, [])
    gate = first_stage(0, [])
    join(2, gate)
    gate = first_stage(1, gate)
    ready = first_stage(2, gate)
    share_with_core(0, ready)
    gate = ready + second_stage(0, ready)
    ready = first_stage(3, gate)
    share_with_core(1, ready)
    gate = ready + second_stage(1, ready)
    ready = first_stage(4, gate)
    share_with_core(2, ready)
    gate = ready + second_stage(2, ready) + third_stage(0, ready)
    ready = gate = first_stage(5, gate)
    gate = ready + second_stage(3, ready) + third_stage(1, ready)
    ready = rows_of_input_grad(GRAD_PARTS[0], gate)
    gate = ready + second_stage(4, ready) + second_stage(5, ready) + third_stage(2, ready)
    ready = rows_of_input_grad(GRAD_PARTS[1], gate)
    gate = ready + third_stage(3, ready) + third_stage(4, ready) + third_stage(5, ready)
    ready = rows_of_input_grad(GRAD_PARTS[2], gate)
    for at in range(6):
        last_stage(at, ready)
    mine = z_high == half
    grad_weight = jnp.stack(
        [jnp.where(mine, result[branch], result[3 + branch]) for branch in range(3)]
    )
    grad_input = row_parts[-1].reshape(rows_dev, cols, local_chan)
    return grad_input, grad_weight * grad_scale


def general(features, grad_out, pre_act, weights):
    rows_dev, cols, local_chan = features.shape
    out_chan = weights.shape[2]
    masked = grad_out * (pre_act > 0).astype(jnp.bfloat16)
    own_rows = lax.all_gather(masked, "chan", axis=2, tiled=True)
    kernels = weights.reshape(3, 9 * out_chan, local_chan)
    grad_input = jnp.zeros((rows_dev, cols, local_chan), jnp.float32)
    kernel_list = []
    for branch, dilation in enumerate(RATES):
        tap_list = []
        for row_step in (-1, 0, 1):
            rows = own_rows[branch]
            if row_step:
                rows = jnp.concatenate(fetch(rows, -row_step, dilation))
            padded = jnp.pad(rows, ((0, 0), (0, 0), (dilation, dilation)))
            for col_step in (-1, 0, 1):
                cols_at = dilation - col_step * dilation
                tap_list.append(padded[:, :, cols_at : cols_at + cols])
        stacked_taps = jnp.concatenate(tap_list, axis=1)
        grad_input = grad_input + jnp.einsum(
            "rkc,ki->rci", stacked_taps, kernels[branch], preferred_element_type=jnp.float32
        )
        kernel_list.append(
            jnp.einsum("rkc,rci->ki", stacked_taps, features, preferred_element_type=jnp.float32)
        )
    partial_grad = jnp.stack(kernel_list, axis=0).reshape(3, 9, out_chan, local_chan)
    summed = lax.psum_scatter(partial_grad, "rows", scatter_dimension=2, tiled=True)
    return (grad_input.astype(jnp.bfloat16), summed * grad_scale)


def solution(mesh):
    in_specs = (
        P("rows", None, "chan"),
        P(None, "rows", "chan", None),
        P(None, "rows", "chan", None),
        P(None, None, None, "chan"),
    )
    out_specs = (P("rows", None, "chan"), P(None, None, "rows", "chan"))
    fast = mesh.shape["rows"] == 16 and mesh.shape["chan"] == 2
    if not fast:
        return jax.shard_map(
            general, mesh=mesh, in_specs=in_specs, out_specs=out_specs, check_vma=False
        )

    return jax.shard_map(shards, mesh=mesh, in_specs=in_specs, out_specs=out_specs, check_vma=False)
```

```python
import functools

import jax
import jax.numpy as jnp
from jax import lax
from jax.experimental import pallas as pl
from jax.experimental.pallas import tpu as pltpu
from jax.sharding import PartitionSpec as P

RATES = (12, 24, 36)
grad_scale = 0.00390625
TOGETHER = 2
GRAD_PARTS = (2, 2, 4)


def passed_along(array, axis, by):
    count = lax.axis_size(axis)
    pairs = [(i, i + by) for i in range(count) if 0 <= i + by < count]
    return lax.ppermute(array, axis, pairs)


def swapped(array, axis, bit):
    count = lax.axis_size(axis)
    return lax.ppermute(array, axis, [(i, i ^ bit) for i in range(count)])


def row_pieces(dilation, side, rows_dev):
    start_strip = side * dilation // rows_dev
    remainder = side * dilation % rows_dev
    if remainder == 0:
        return [(start_strip, 0, rows_dev)]
    return [(start_strip, remainder, rows_dev), (start_strip + 1, 0, remainder)]


def fetch(source, side, dilation):
    return [
        passed_along(source[low:high], "rows", -strip)
        for strip, low, high in row_pieces(dilation, side, source.shape[0])
    ]


def after(values, gate):
    return lax.optimization_barrier((values, gate))[0]


def moved(tile, shift, axis):
    if shift == 0:
        return tile
    size = tile.shape[axis]
    at = lax.broadcasted_iota(jnp.int32, tile.shape, axis)
    keep = at >= shift if shift > 0 else at < size + shift
    return jnp.where(keep, pltpu.roll(tile, shift % size, axis), jnp.zeros_like(tile))


def joined(pieces):
    if len({piece.shape for piece in pieces}) == 1:
        stacked = jnp.stack(pieces)
        return stacked.reshape((-1,) + stacked.shape[2:])
    return jnp.concatenate(pieces)


def kernel_grad_body(branch, dilation, bits_ref, own, pair, own_far, pair_far, feats,
                     feats_far, keep_out, send_out, taps_near, taps_far, sums):
    _, rows_dev, low, _, _, lanes, cols = own.shape
    core, first = bits_ref[0], bits_ref[1]

    def build(own_ref, pair_ref, turn, target):
        for row in range(TOGETHER):
            at_row = turn * TOGETHER + row
            for part in range(2):
                bit = first if part == 0 else 1 - first
                for row_step in range(3):
                    for group in range(low):
                        place = (group, bit, core)
                        if row_step == 1:
                            tile = own_ref[(branch, at_row) + place]
                        else:
                            tile = pair_ref[(row_step // 2, at_row) + place]
                        for step in (-1, 0, 1):
                            tap = row_step * 3 + step + 1
                            at = ((part * low + group) * 9 + tap) * lanes
                            target[at : at + lanes, row * cols : (row + 1) * cols] = moved(
                                tile, step * dilation, 1
                            )

    build(own, pair, 0, taps_near)
    sums[...] = jnp.zeros_like(sums)
    turns = rows_dev // TOGETHER

    def step(turn, carry):
        rows = pl.ds(pl.multiple_of(turn * TOGETHER * cols, TOGETHER * cols), TOGETHER * cols)
        sums[...] += jnp.dot(
            taps_near[...], feats[rows, :], preferred_element_type=jnp.float32
        )
        build(own_far, pair_far, turn, taps_far)
        sums[...] += jnp.dot(taps_far[...], feats_far[rows, :], preferred_element_type=jnp.float32)
        build(own, pair, jnp.minimum(turn + 1, turns - 1), taps_near)
        return carry

    lax.fori_loop(0, turns, step, 0)
    size = keep_out.shape[0]
    keep_out[...] = sums[:size]
    send_out[...] = sums[size:]


def kernel_grad(bits, near, far, feats, feats_far, branch, lanes):
    own, pair = near
    rows_dev, half_out, cols = own.shape[1:]
    chan = feats.shape[1]
    split = lambda a: a.reshape(a.shape[0], rows_dev, 2, 2, 2, lanes, cols)
    vmem = pl.BlockSpec(memory_space=pltpu.VMEM)
    depth = 9 * half_out // 2
    shape = jax.ShapeDtypeStruct((depth // 2, chan), jnp.float32)
    keep, send = pl.pallas_call(
        functools.partial(kernel_grad_body, branch, RATES[branch]),
        in_specs=[pl.BlockSpec(memory_space=pltpu.SMEM)] + [vmem] * 6,
        out_specs=[vmem, vmem],
        out_shape=[shape, shape],
        scratch_shapes=[
            pltpu.VMEM((depth, TOGETHER * cols), own.dtype),
            pltpu.VMEM((depth, TOGETHER * cols), own.dtype),
            pltpu.VMEM((depth, chan), jnp.float32),
        ],
        compiler_params=pltpu.CompilerParams(vmem_limit_bytes=20 << 20),
        cost_estimate=pl.CostEstimate(
            flops=4 * depth * rows_dev * cols * chan,
            transcendentals=0,
            bytes_accessed=4 * feats.size + 4 * depth * chan,
        ),
        name="kernel_grad",
    )(bits, split(own), split(pair), split(far[0]), split(far[1]), feats, feats_far)
    view = lambda a: a.reshape(2, 9, lanes, chan)
    return view(keep), view(send)


def input_grad_body(together, first_row, half_ref, own, own_other, *refs):
    pairs, weights, (out, taps) = refs[:6], refs[6], refs[-2:]
    turn = pl.program_id(0)
    turns = pl.num_programs(0)
    half_out, cols = own.shape[2:]
    half = half_ref[0]
    count = weights.shape[0]

    def build(branch, at_turn):
        for row in range(together):
            at_row = first_row + at_turn * together + row
            for which in range(2):
                place = half if which == 0 else 1 - half
                for row_step in range(3):
                    if row_step == 1:
                        tile = (own, own_other)[which][branch, at_row]
                    else:
                        tile = pairs[2 * branch + which][row_step // 2, at_row]
                    turned = tile.T
                    for step in (-1, 0, 1):
                        tap = row_step * 3 + step + 1
                        at = pl.multiple_of((tap * 2 + place) * half_out, half_out)
                        taps[branch, row * cols : (row + 1) * cols, pl.ds(at, half_out)] = moved(
                            turned, step * RATES[branch], 0
                        )

    @pl.when(turn == 0)
    def _():
        build(0, 0)

    total = None
    for branch in range(count):
        part = jnp.dot(taps[branch], weights[branch], preferred_element_type=jnp.float32)
        total = part if total is None else total + part
        if branch + 1 < count:
            build(branch + 1, turn)
        else:
            build(0, jnp.minimum(turn + 1, turns - 1))
    out[...] = total.astype(out.dtype)


def input_grad(half, own, own_other, pairs, weights, first_row, rows, before, together=1):
    rows_dev, _, cols = own.shape[1:]
    count, depth, chan = weights.shape
    vmem = pl.BlockSpec(memory_space=pltpu.VMEM)
    operands = (half, own, own_other, *pairs, weights) + before
    return pl.pallas_call(
        functools.partial(input_grad_body, together, first_row),
        grid=(rows // together,),
        in_specs=[pl.BlockSpec(memory_space=pltpu.SMEM)]
        + [vmem] * 9
        + [pl.BlockSpec(memory_space=pl.ANY)] * len(before),
        out_specs=pl.BlockSpec(
            (together * cols, chan), lambda turn: (turn + first_row // together, 0)
        ),
        input_output_aliases={10: 0} if before else {},
        scratch_shapes=[
            pltpu.VMEM((count, together * cols, depth), own.dtype),
        ],
        out_shape=jax.ShapeDtypeStruct((rows_dev * cols, chan), jnp.bfloat16),
        compiler_params=pltpu.CompilerParams(vmem_limit_bytes=20 << 20),
        cost_estimate=pl.CostEstimate(
            flops=2 * rows * cols * count * depth * chan,
            transcendentals=0,
            bytes_accessed=2 * weights.size + 2 * rows * cols * chan,
        ),
        name="input_grad",
    )(*operands)


def partial_bound(features, masked):
    wide = masked.astype(jnp.float32)
    mask_power = jnp.broadcast_to(jnp.max(jnp.sum(wide * wide, axis=(1, 3))), (8, 128))
    mask_power = jnp.maximum(mask_power, swapped(mask_power, "chan", 1))
    wide = features.astype(jnp.float32)
    feat_power = jnp.max(jnp.sum(wide * wide, axis=(0, 1)))
    upper = lax.broadcasted_iota(jnp.int32, (8, 128), 0) < 4
    both = jnp.where(upper, feat_power, mask_power)
    bit = 1
    while bit < lax.axis_size("rows"):
        both = both + swapped(both, "rows", bit)
        bit *= 2
    return jnp.maximum(jnp.sqrt(both[0, 0]) * jnp.sqrt(both[4, 0]) * 1.01, 1e-30)


def shards(features, grad_out, pre_act, weights):
    rows_dev, cols, local_chan = features.shape
    out_chan = weights.shape[2]
    strips = lax.axis_size("rows")
    lanes = out_chan // strips
    place = lax.axis_index("rows")
    half = lax.axis_index("chan")
    core, y_at, z_low, z_high = place % 2, place // 2 % 2, place // 4 % 2, place // 8
    bits = jnp.stack([core, y_at]).astype(jnp.int32)
    half_arg = half.astype(jnp.int32).reshape(1)
    kernels = weights.reshape(3, 9 * out_chan, local_chan)
    masked = jnp.where(pre_act > 0, grad_out, jnp.zeros_like(grad_out))
    feats = features.reshape(rows_dev * cols, local_chan)
    feats_far = swapped(feats, "rows", 1)
    bound = partial_bound(features, masked)
    grow, shrink = 32000.0 / bound, bound / 32000.0

    own = [masked, swapped(masked, "chan", 1)]
    pieces = []
    for branch, dilation in enumerate(RATES):
        pieces.append(fetch(masked[branch], 1, dilation) + fetch(masked[branch], -1, dilation))
    own_far = [swapped(own[0], "rows", 1), None]
    pairs, pairs_far = [[None] * 3, [None] * 3], [[None] * 3, [None] * 3]

    def join(branch, gate):
        pair = joined(after(pieces[branch], gate)).reshape((2,) + masked.shape[1:])
        pair = lax.optimization_barrier(pair)
        pairs[1][branch] = swapped(pair, "chan", 1)
        pairs[0][branch] = pair
        pairs_far[0][branch] = swapped(pair, "rows", 1)

    def share_with_core(branch, gate):
        if branch == 0:
            own_far[1] = swapped(after(own[1], gate), "rows", 1)
        pairs_far[1][branch] = swapped(after(pairs[1][branch], gate), "rows", 1)


    def pack(values):
        return (values * grow).astype(jnp.float16)

    def unpack(values):
        return values.astype(jnp.float32) * shrink

    steps = [(share, branch) for share in range(2) for branch in range(3)]
    state, result = {}, {}

    def first_stage(at, gate):
        share, branch = steps[at]
        keep, send = kernel_grad(
            after(bits, gate),
            (own[share], pairs[share][branch]),
            (own_far[share], pairs_far[share][branch]),
            feats,
            feats_far,
            branch,
            lanes,
        )
        send = pack(send)
        state[at] = (keep, swapped(send, "rows", 2))
        return [send, keep]

    def second_stage(at, gate):
        keep, got = after(state[at], gate)
        total = keep + unpack(got)
        send = pack(lax.dynamic_index_in_dim(total, 1 - z_low, 0, keepdims=False))
        keep = lax.dynamic_index_in_dim(total, z_low, 0, keepdims=False)
        state[at] = (keep, swapped(send, "rows", 4))
        return [send, keep]

    def third_stage(at, gate):
        share = steps[at][0]
        keep, got = after(state[at], gate)
        total = keep + unpack(got)
        pairs = [
            (row * 2 + chan, (row ^ 8) * 2 + chan)
            for row in range(strips)
            for chan in range(2)
            if row // 8 != (chan if share == 0 else 1 - chan)
        ]
        send = pack(total)
        state[at] = (total, lax.ppermute(send, ("rows", "chan"), pairs))
        return [send, total]

    def last_stage(at, gate):
        keep, got = after(state[at], gate)
        result[at] = keep + unpack(got)
        return [result[at]]

    row_parts = []
    first_row = 0

    def rows_of_input_grad(count, gate):
        nonlocal first_row
        flat = [pairs[share][branch] for branch in range(3) for share in range(2)]
        part = input_grad(
            after(half_arg, gate),
            own[0],
            own[1],
            flat,
            kernels,
            first_row,
            count,
            tuple(row_parts[-1:]),
        )
        row_parts.append(part)
        first_row += count
        return [row_parts[-1]]

    join(0, [])
    join(1, [])
    gate = first_stage(0, [])
    join(2, gate)
    gate = first_stage(1, gate)
    ready = first_stage(2, gate)
    share_with_core(0, ready)
    gate = ready + second_stage(0, ready)
    ready = first_stage(3, gate)
    share_with_core(1, ready)
    gate = ready + second_stage(1, ready)
    ready = first_stage(4, gate)
    share_with_core(2, ready)
    gate = ready + second_stage(2, ready) + third_stage(0, ready) + second_stage(3, ready)
    ready = first_stage(5, gate)
    gate = ready + third_stage(1, ready) + second_stage(4, ready) + third_stage(2, ready)
    ready = rows_of_input_grad(GRAD_PARTS[0], gate)
    gate = ready + second_stage(5, ready) + third_stage(3, ready)
    ready = rows_of_input_grad(GRAD_PARTS[1], gate)
    gate = ready + third_stage(4, ready) + third_stage(5, ready)
    ready = rows_of_input_grad(GRAD_PARTS[2], gate)
    for at in range(6):
        last_stage(at, ready)
    mine = z_high == half
    grad_weight = jnp.stack(
        [jnp.where(mine, result[branch], result[3 + branch]) for branch in range(3)]
    )
    grad_input = row_parts[-1].reshape(rows_dev, cols, local_chan)
    return grad_input, grad_weight * grad_scale


def general(features, grad_out, pre_act, weights):
    rows_dev, cols, local_chan = features.shape
    out_chan = weights.shape[2]
    masked = grad_out * (pre_act > 0).astype(jnp.bfloat16)
    own_rows = lax.all_gather(masked, "chan", axis=2, tiled=True)
    kernels = weights.reshape(3, 9 * out_chan, local_chan)
    grad_input = jnp.zeros((rows_dev, cols, local_chan), jnp.float32)
    kernel_list = []
    for branch, dilation in enumerate(RATES):
        tap_list = []
        for row_step in (-1, 0, 1):
            rows = own_rows[branch]
            if row_step:
                rows = jnp.concatenate(fetch(rows, -row_step, dilation))
            padded = jnp.pad(rows, ((0, 0), (0, 0), (dilation, dilation)))
            for col_step in (-1, 0, 1):
                cols_at = dilation - col_step * dilation
                tap_list.append(padded[:, :, cols_at : cols_at + cols])
        stacked_taps = jnp.concatenate(tap_list, axis=1)
        grad_input = grad_input + jnp.einsum(
            "rkc,ki->rci", stacked_taps, kernels[branch], preferred_element_type=jnp.float32
        )
        kernel_list.append(
            jnp.einsum("rkc,rci->ki", stacked_taps, features, preferred_element_type=jnp.float32)
        )
    partial_grad = jnp.stack(kernel_list, axis=0).reshape(3, 9, out_chan, local_chan)
    summed = lax.psum_scatter(partial_grad, "rows", scatter_dimension=2, tiled=True)
    return (grad_input.astype(jnp.bfloat16), summed * grad_scale)


def solution(mesh):
    in_specs = (
        P("rows", None, "chan"),
        P(None, "rows", "chan", None),
        P(None, "rows", "chan", None),
        P(None, None, None, "chan"),
    )
    out_specs = (P("rows", None, "chan"), P(None, None, "rows", "chan"))
    fast = mesh.shape["rows"] == 16 and mesh.shape["chan"] == 2
    if not fast:
        return jax.shard_map(
            general, mesh=mesh, in_specs=in_specs, out_specs=out_specs, check_vma=False
        )

    return jax.shard_map(shards, mesh=mesh, in_specs=in_specs, out_specs=out_specs, check_vma=False)
```

```python
import functools

import jax
import jax.numpy as jnp
from jax import lax
from jax.experimental import pallas as pl
from jax.experimental.pallas import tpu as pltpu
from jax.sharding import PartitionSpec as P

RATES = (12, 24, 36)
grad_scale = 0.00390625
TOGETHER = 2
GRAD_PARTS = (2, 2, 4)


def passed_along(array, axis, by):
    count = lax.axis_size(axis)
    pairs = [(i, i + by) for i in range(count) if 0 <= i + by < count]
    return lax.ppermute(array, axis, pairs)


def swapped(array, axis, bit):
    count = lax.axis_size(axis)
    return lax.ppermute(array, axis, [(i, i ^ bit) for i in range(count)])


def row_pieces(dilation, side, rows_dev):
    start_strip = side * dilation // rows_dev
    remainder = side * dilation % rows_dev
    if remainder == 0:
        return [(start_strip, 0, rows_dev)]
    return [(start_strip, remainder, rows_dev), (start_strip + 1, 0, remainder)]


def fetch(source, side, dilation):
    return [
        passed_along(source[low:high], "rows", -strip)
        for strip, low, high in row_pieces(dilation, side, source.shape[0])
    ]


def after(values, gate):
    return lax.optimization_barrier((values, gate))[0]


def moved(tile, shift, axis):
    if shift == 0:
        return tile
    size = tile.shape[axis]
    at = lax.broadcasted_iota(jnp.int32, tile.shape, axis)
    keep = at >= shift if shift > 0 else at < size + shift
    return jnp.where(keep, pltpu.roll(tile, shift % size, axis), jnp.zeros_like(tile))


def joined(pieces):
    if len({piece.shape for piece in pieces}) == 1:
        stacked = jnp.stack(pieces)
        return stacked.reshape((-1,) + stacked.shape[2:])
    return jnp.concatenate(pieces)


def kernel_grad_body(branch, dilation, bits_ref, own_hbm, pair_hbm, own_far_hbm, pair_far_hbm,
                     feats_hbm, feats_far_hbm, keep_out, send_out, own, pair, feats, taps_near,
                     taps_far, sums, row_sems, feat_sems):
    _, rows_dev, low, _, _, lanes, cols = own.shape
    core, first = bits_ref[0], bits_ref[1]
    turns = rows_dev // TOGETHER
    span = TOGETHER * cols
    near_loads = (
        pltpu.make_async_copy(own_hbm.at[branch], own.at[0], row_sems.at[0]),
        pltpu.make_async_copy(pair_hbm, pair.at[0], row_sems.at[1]),
    )
    far_loads = (
        pltpu.make_async_copy(own_far_hbm.at[branch], own.at[1], row_sems.at[2]),
        pltpu.make_async_copy(pair_far_hbm, pair.at[1], row_sems.at[3]),
    )

    def feat_load(which, turn):
        rows = pl.ds(pl.multiple_of(turn * span, span), span)
        source = (feats_hbm, feats_far_hbm)[which]
        return pltpu.make_async_copy(
            source.at[rows], feats.at[which, rows], feat_sems.at[which, turn]
        )

    for load in near_loads:
        load.start()
    feat_load(0, 0).start()
    for load in near_loads:
        load.wait()
    for load in far_loads:
        load.start()
    feat_load(1, 0).start()
    for turn in range(1, turns):
        feat_load(0, turn).start()
        feat_load(1, turn).start()

    def build(which, turn, target):
        for row in range(TOGETHER):
            at_row = turn * TOGETHER + row
            for part in range(2):
                bit = first if part == 0 else 1 - first
                for row_step in range(3):
                    for group in range(low):
                        place = (group, bit, core)
                        if row_step == 1:
                            tile = own[(which, at_row) + place]
                        else:
                            tile = pair[(which, row_step // 2, at_row) + place]
                        for step in (-1, 0, 1):
                            tap = row_step * 3 + step + 1
                            at = ((part * low + group) * 9 + tap) * lanes
                            target[at : at + lanes, row * cols : (row + 1) * cols] = moved(
                                tile, step * dilation, 1
                            )

    build(0, 0, taps_near)
    sums[...] = jnp.zeros_like(sums)
    for load in far_loads:
        load.wait()

    def step(turn, carry):
        rows = pl.ds(pl.multiple_of(turn * span, span), span)
        feat_load(0, turn).wait()
        feat_load(1, turn).wait()
        sums[...] += jnp.dot(
            taps_near[...], feats[0, rows, :], preferred_element_type=jnp.float32
        )
        build(1, turn, taps_far)
        sums[...] += jnp.dot(taps_far[...], feats[1, rows, :], preferred_element_type=jnp.float32)
        build(0, jnp.minimum(turn + 1, turns - 1), taps_near)
        return carry

    lax.fori_loop(0, turns, step, 0)
    size = keep_out.shape[0]
    keep_out[...] = sums[:size]
    send_out[...] = sums[size:]


def kernel_grad(bits, near, far, feats, feats_far, branch, lanes):
    own, pair = near
    rows_dev, half_out, cols = own.shape[1:]
    chan = feats.shape[1]
    vmem = pl.BlockSpec(memory_space=pltpu.VMEM)
    hbm = pl.BlockSpec(memory_space=pl.ANY)
    depth = 9 * half_out // 2
    shares = (rows_dev, 2, 2, 2, lanes, cols)
    split = lambda a: a.reshape((a.shape[0],) + shares)
    shape = jax.ShapeDtypeStruct((depth // 2, chan), jnp.float32)
    keep, send = pl.pallas_call(
        functools.partial(kernel_grad_body, branch, RATES[branch]),
        in_specs=[pl.BlockSpec(memory_space=pltpu.SMEM)] + [hbm] * 6,
        out_specs=[vmem, vmem],
        out_shape=[shape, shape],
        scratch_shapes=[
            pltpu.VMEM((2,) + shares, own.dtype),
            pltpu.VMEM((2, 2) + shares, own.dtype),
            pltpu.VMEM((2,) + feats.shape, feats.dtype),
            pltpu.VMEM((depth, TOGETHER * cols), own.dtype),
            pltpu.VMEM((depth, TOGETHER * cols), own.dtype),
            pltpu.VMEM((depth, chan), jnp.float32),
            pltpu.SemaphoreType.DMA((4,)),
            pltpu.SemaphoreType.DMA((2, rows_dev // TOGETHER)),
        ],
        compiler_params=pltpu.CompilerParams(vmem_limit_bytes=24 << 20),
        cost_estimate=pl.CostEstimate(
            flops=4 * depth * rows_dev * cols * chan,
            transcendentals=0,
            bytes_accessed=4 * feats.size + 4 * depth * chan,
        ),
        name="kernel_grad",
    )(bits, split(own), split(pair), split(far[0]), split(far[1]), feats, feats_far)
    view = lambda a: a.reshape(2, 9, lanes, chan)
    return view(keep), view(send)


def input_grad_body(together, first_row, half_ref, *refs):
    sources, weights, (out, own, pairs, taps, sems) = refs[:8], refs[8], refs[-5:]
    turn = pl.program_id(0)
    turns = pl.num_programs(0)
    rows, half_out, cols = own.shape[2:]
    half = half_ref[0]
    count = weights.shape[0]
    targets = [own.at[at] for at in range(2)] + [pairs.at[at] for at in range(6)]
    loads = [
        pltpu.make_async_copy(source.at[:, pl.ds(first_row, rows)], target, sems.at[at])
        for at, (source, target) in enumerate(zip(sources, targets))
    ]

    def build(branch, at_turn):
        for row in range(together):
            at_row = at_turn * together + row
            for which in range(2):
                place = half if which == 0 else 1 - half
                for row_step in range(3):
                    if row_step == 1:
                        tile = own[which, branch, at_row]
                    else:
                        tile = pairs[2 * branch + which, row_step // 2, at_row]
                    turned = tile.T
                    for step in (-1, 0, 1):
                        tap = row_step * 3 + step + 1
                        at = pl.multiple_of((tap * 2 + place) * half_out, half_out)
                        taps[branch, row * cols : (row + 1) * cols, pl.ds(at, half_out)] = moved(
                            turned, step * RATES[branch], 0
                        )

    @pl.when(turn == 0)
    def _():
        for load in loads:
            load.start()
        for load in loads:
            load.wait()
        build(0, 0)

    total = None
    for branch in range(count):
        part = jnp.dot(taps[branch], weights[branch], preferred_element_type=jnp.float32)
        total = part if total is None else total + part
        if branch + 1 < count:
            build(branch + 1, turn)
        else:
            build(0, jnp.minimum(turn + 1, turns - 1))
    out[...] = total.astype(out.dtype)


def input_grad(half, own, own_other, pairs, weights, first_row, rows, before, together=1):
    rows_dev, half_out, cols = own.shape[1:]
    count, depth, chan = weights.shape
    vmem = pl.BlockSpec(memory_space=pltpu.VMEM)
    hbm = pl.BlockSpec(memory_space=pl.ANY)
    operands = (half, own, own_other, *pairs, weights) + before
    return pl.pallas_call(
        functools.partial(input_grad_body, together, first_row),
        grid=(rows // together,),
        in_specs=[pl.BlockSpec(memory_space=pltpu.SMEM)]
        + [hbm] * 8
        + [vmem]
        + [hbm] * len(before),
        out_specs=pl.BlockSpec(
            (together * cols, chan), lambda turn: (turn + first_row // together, 0)
        ),
        input_output_aliases={10: 0} if before else {},
        scratch_shapes=[
            pltpu.VMEM((2, count, rows, half_out, cols), own.dtype),
            pltpu.VMEM((2 * count, 2, rows, half_out, cols), own.dtype),
            pltpu.VMEM((count, together * cols, depth), own.dtype),
            pltpu.SemaphoreType.DMA((8,)),
        ],
        out_shape=jax.ShapeDtypeStruct((rows_dev * cols, chan), jnp.bfloat16),
        compiler_params=pltpu.CompilerParams(vmem_limit_bytes=24 << 20),
        cost_estimate=pl.CostEstimate(
            flops=2 * rows * cols * count * depth * chan,
            transcendentals=0,
            bytes_accessed=2 * weights.size + 2 * rows * cols * chan,
        ),
        name="input_grad",
    )(*operands)


def partial_bound(features, masked):
    wide = masked.astype(jnp.float32)
    mask_power = jnp.broadcast_to(jnp.max(jnp.sum(wide * wide, axis=(1, 3))), (8, 128))
    mask_power = jnp.maximum(mask_power, swapped(mask_power, "chan", 1))
    wide = features.astype(jnp.float32)
    feat_power = jnp.max(jnp.sum(wide * wide, axis=(0, 1)))
    upper = lax.broadcasted_iota(jnp.int32, (8, 128), 0) < 4
    both = jnp.where(upper, feat_power, mask_power)
    bit = 1
    while bit < lax.axis_size("rows"):
        both = both + swapped(both, "rows", bit)
        bit *= 2
    return jnp.maximum(jnp.sqrt(both[0, 0]) * jnp.sqrt(both[4, 0]) * 1.01, 1e-30)


def shards(features, grad_out, pre_act, weights):
    rows_dev, cols, local_chan = features.shape
    out_chan = weights.shape[2]
    strips = lax.axis_size("rows")
    lanes = out_chan // strips
    place = lax.axis_index("rows")
    half = lax.axis_index("chan")
    core, y_at, z_low, z_high = place % 2, place // 2 % 2, place // 4 % 2, place // 8
    bits = jnp.stack([core, y_at]).astype(jnp.int32)
    half_arg = half.astype(jnp.int32).reshape(1)
    kernels = weights.reshape(3, 9 * out_chan, local_chan)
    masked = jnp.where(pre_act > 0, grad_out, jnp.zeros_like(grad_out))
    feats = features.reshape(rows_dev * cols, local_chan)
    feats_far = swapped(feats, "rows", 1)
    bound = partial_bound(features, masked)
    grow, shrink = 32000.0 / bound, bound / 32000.0

    own = [masked, swapped(masked, "chan", 1)]
    pieces = []
    for branch, dilation in enumerate(RATES):
        pieces.append(fetch(masked[branch], 1, dilation) + fetch(masked[branch], -1, dilation))
    own_far = [swapped(own[0], "rows", 1), None]
    pairs, pairs_far = [[None] * 3, [None] * 3], [[None] * 3, [None] * 3]

    def join(branch, gate):
        pair = joined(after(pieces[branch], gate)).reshape((2,) + masked.shape[1:])
        pair = lax.optimization_barrier(pair)
        pairs[1][branch] = swapped(pair, "chan", 1)
        pairs[0][branch] = pair
        pairs_far[0][branch] = swapped(pair, "rows", 1)

    def share_with_core(branch, gate):
        if branch == 0:
            own_far[1] = swapped(after(own[1], gate), "rows", 1)
        pairs_far[1][branch] = swapped(after(pairs[1][branch], gate), "rows", 1)


    def pack(values):
        return (values * grow).astype(jnp.float16)

    def unpack(values):
        return values.astype(jnp.float32) * shrink

    steps = [(share, branch) for share in range(2) for branch in range(3)]
    state, result = {}, {}

    def first_stage(at, gate):
        share, branch = steps[at]
        keep, send = kernel_grad(
            after(bits, gate),
            (own[share], pairs[share][branch]),
            (own_far[share], pairs_far[share][branch]),
            feats,
            feats_far,
            branch,
            lanes,
        )
        send = pack(send)
        state[at] = (keep, swapped(send, "rows", 2))
        return [send, keep]

    def second_stage(at, gate):
        keep, got = after(state[at], gate)
        total = keep + unpack(got)
        send = pack(lax.dynamic_index_in_dim(total, 1 - z_low, 0, keepdims=False))
        keep = lax.dynamic_index_in_dim(total, z_low, 0, keepdims=False)
        state[at] = (keep, swapped(send, "rows", 4))
        return [send, keep]

    def third_stage(at, gate):
        share = steps[at][0]
        keep, got = after(state[at], gate)
        total = keep + unpack(got)
        pairs = [
            (row * 2 + chan, (row ^ 8) * 2 + chan)
            for row in range(strips)
            for chan in range(2)
            if row // 8 != (chan if share == 0 else 1 - chan)
        ]
        send = pack(total)
        state[at] = (total, lax.ppermute(send, ("rows", "chan"), pairs))
        return [send, total]

    def last_stage(at, gate):
        keep, got = after(state[at], gate)
        result[at] = keep + unpack(got)
        return [result[at]]

    row_parts = []
    first_row = 0

    def rows_of_input_grad(count, gate):
        nonlocal first_row
        flat = [pairs[share][branch] for branch in range(3) for share in range(2)]
        part = input_grad(
            after(half_arg, gate),
            own[0],
            own[1],
            flat,
            kernels,
            first_row,
            count,
            tuple(row_parts[-1:]),
        )
        row_parts.append(part)
        first_row += count
        return [row_parts[-1]]

    join(0, [])
    join(1, [])
    gate = first_stage(0, [])
    join(2, gate)
    gate = first_stage(1, gate)
    ready = first_stage(2, gate)
    share_with_core(0, ready)
    gate = ready + second_stage(0, ready)
    ready = first_stage(3, gate)
    share_with_core(1, ready)
    gate = ready + second_stage(1, ready)
    ready = first_stage(4, gate)
    share_with_core(2, ready)
    gate = ready + second_stage(2, ready) + third_stage(0, ready) + second_stage(3, ready)
    ready = first_stage(5, gate)
    gate = ready + third_stage(1, ready) + second_stage(4, ready) + third_stage(2, ready)
    ready = rows_of_input_grad(GRAD_PARTS[0], gate)
    gate = ready + second_stage(5, ready) + third_stage(3, ready)
    ready = rows_of_input_grad(GRAD_PARTS[1], gate)
    gate = ready + third_stage(4, ready) + third_stage(5, ready)
    ready = rows_of_input_grad(GRAD_PARTS[2], gate)
    for at in range(6):
        last_stage(at, ready)
    mine = z_high == half
    grad_weight = jnp.stack(
        [jnp.where(mine, result[branch], result[3 + branch]) for branch in range(3)]
    )
    grad_input = row_parts[-1].reshape(rows_dev, cols, local_chan)
    return grad_input, grad_weight * grad_scale


def general(features, grad_out, pre_act, weights):
    rows_dev, cols, local_chan = features.shape
    out_chan = weights.shape[2]
    masked = grad_out * (pre_act > 0).astype(jnp.bfloat16)
    own_rows = lax.all_gather(masked, "chan", axis=2, tiled=True)
    kernels = weights.reshape(3, 9 * out_chan, local_chan)
    grad_input = jnp.zeros((rows_dev, cols, local_chan), jnp.float32)
    kernel_list = []
    for branch, dilation in enumerate(RATES):
        tap_list = []
        for row_step in (-1, 0, 1):
            rows = own_rows[branch]
            if row_step:
                rows = jnp.concatenate(fetch(rows, -row_step, dilation))
            padded = jnp.pad(rows, ((0, 0), (0, 0), (dilation, dilation)))
            for col_step in (-1, 0, 1):
                cols_at = dilation - col_step * dilation
                tap_list.append(padded[:, :, cols_at : cols_at + cols])
        stacked_taps = jnp.concatenate(tap_list, axis=1)
        grad_input = grad_input + jnp.einsum(
            "rkc,ki->rci", stacked_taps, kernels[branch], preferred_element_type=jnp.float32
        )
        kernel_list.append(
            jnp.einsum("rkc,rci->ki", stacked_taps, features, preferred_element_type=jnp.float32)
        )
    partial_grad = jnp.stack(kernel_list, axis=0).reshape(3, 9, out_chan, local_chan)
    summed = lax.psum_scatter(partial_grad, "rows", scatter_dimension=2, tiled=True)
    return (grad_input.astype(jnp.bfloat16), summed * grad_scale)


def solution(mesh):
    in_specs = (
        P("rows", None, "chan"),
        P(None, "rows", "chan", None),
        P(None, "rows", "chan", None),
        P(None, None, None, "chan"),
    )
    out_specs = (P("rows", None, "chan"), P(None, None, "rows", "chan"))
    fast = mesh.shape["rows"] == 16 and mesh.shape["chan"] == 2
    if not fast:
        return jax.shard_map(
            general, mesh=mesh, in_specs=in_specs, out_specs=out_specs, check_vma=False
        )

    return jax.shard_map(shards, mesh=mesh, in_specs=in_specs, out_specs=out_specs, check_vma=False)
```

```python
import functools

import jax
import jax.numpy as jnp
from jax import lax
from jax.experimental import pallas as pl
from jax.experimental.pallas import tpu as pltpu
from jax.sharding import PartitionSpec as P

RATES = (12, 24, 36)
grad_scale = 0.00390625
TOGETHER = 2
GRAD_PARTS = (2, 2, 4)


def passed_along(array, axis, by):
    count = lax.axis_size(axis)
    pairs = [(i, i + by) for i in range(count) if 0 <= i + by < count]
    return lax.ppermute(array, axis, pairs)


def swapped(array, axis, bit):
    count = lax.axis_size(axis)
    return lax.ppermute(array, axis, [(i, i ^ bit) for i in range(count)])


def row_pieces(dilation, side, rows_dev):
    start_strip = side * dilation // rows_dev
    remainder = side * dilation % rows_dev
    if remainder == 0:
        return [(start_strip, 0, rows_dev)]
    return [(start_strip, remainder, rows_dev), (start_strip + 1, 0, remainder)]


def fetch(source, side, dilation):
    return [
        passed_along(source[low:high], "rows", -strip)
        for strip, low, high in row_pieces(dilation, side, source.shape[0])
    ]


def after(values, gate):
    return lax.optimization_barrier((values, gate))[0]


def moved(tile, shift, axis):
    if shift == 0:
        return tile
    size = tile.shape[axis]
    at = lax.broadcasted_iota(jnp.int32, tile.shape, axis)
    keep = at >= shift if shift > 0 else at < size + shift
    return jnp.where(keep, pltpu.roll(tile, shift % size, axis), jnp.zeros_like(tile))


def joined(pieces):
    if len({piece.shape for piece in pieces}) == 1:
        stacked = jnp.stack(pieces)
        return stacked.reshape((-1,) + stacked.shape[2:])
    return jnp.concatenate(pieces)


def kernel_grad_body(branch, dilation, bits_ref, own_hbm, pair_hbm, own_far_hbm, pair_far_hbm,
                     feats_hbm, feats_far_hbm, keep_out, send_out, own, pair, feats, taps_near,
                     taps_far, sums, row_sems, feat_sems):
    _, rows_dev, low, _, _, lanes, cols = own.shape
    core, first = bits_ref[0], bits_ref[1]
    turns = rows_dev // TOGETHER
    span = TOGETHER * cols
    near_loads = (
        pltpu.make_async_copy(own_hbm.at[branch], own.at[0], row_sems.at[0]),
        pltpu.make_async_copy(pair_hbm, pair.at[0], row_sems.at[1]),
    )
    far_loads = (
        pltpu.make_async_copy(own_far_hbm.at[branch], own.at[1], row_sems.at[2]),
        pltpu.make_async_copy(pair_far_hbm, pair.at[1], row_sems.at[3]),
    )

    def feat_load(which, turn):
        rows = pl.ds(pl.multiple_of(turn * span, span), span)
        source = (feats_hbm, feats_far_hbm)[which]
        return pltpu.make_async_copy(
            source.at[rows], feats.at[which, rows], feat_sems.at[which, turn]
        )

    for load in near_loads:
        load.start()
    feat_load(0, 0).start()
    for load in near_loads:
        load.wait()
    for load in far_loads:
        load.start()
    feat_load(1, 0).start()
    for turn in range(1, turns):
        feat_load(0, turn).start()
        feat_load(1, turn).start()

    def build(which, turn, target):
        for row in range(TOGETHER):
            at_row = turn * TOGETHER + row
            for part in range(2):
                bit = first if part == 0 else 1 - first
                for row_step in range(3):
                    for group in range(low):
                        place = (group, bit, core)
                        if row_step == 1:
                            tile = own[(which, at_row) + place]
                        else:
                            tile = pair[(which, row_step // 2, at_row) + place]
                        for step in (-1, 0, 1):
                            tap = row_step * 3 + step + 1
                            at = ((part * low + group) * 9 + tap) * lanes
                            target[at : at + lanes, row * cols : (row + 1) * cols] = moved(
                                tile, step * dilation, 1
                            )

    build(0, 0, taps_near)
    sums[...] = jnp.zeros_like(sums)
    for load in far_loads:
        load.wait()

    def step(turn, carry):
        rows = pl.ds(pl.multiple_of(turn * span, span), span)
        feat_load(0, turn).wait()
        feat_load(1, turn).wait()
        sums[...] += jnp.dot(
            taps_near[...], feats[0, rows, :], preferred_element_type=jnp.float32
        )
        build(1, turn, taps_far)
        sums[...] += jnp.dot(taps_far[...], feats[1, rows, :], preferred_element_type=jnp.float32)
        build(0, jnp.minimum(turn + 1, turns - 1), taps_near)
        return carry

    lax.fori_loop(0, turns, step, 0)
    size = keep_out.shape[0]
    keep_out[...] = sums[:size]
    send_out[...] = sums[size:]


def kernel_grad(bits, near, far, feats, feats_far, branch, lanes):
    own, pair = near
    rows_dev, half_out, cols = own.shape[1:]
    chan = feats.shape[1]
    vmem = pl.BlockSpec(memory_space=pltpu.VMEM)
    hbm = pl.BlockSpec(memory_space=pl.ANY)
    depth = 9 * half_out // 2
    shares = (rows_dev, 2, 2, 2, lanes, cols)
    split = lambda a: a.reshape((a.shape[0],) + shares)
    shape = jax.ShapeDtypeStruct((depth // 2, chan), jnp.float32)
    keep, send = pl.pallas_call(
        functools.partial(kernel_grad_body, branch, RATES[branch]),
        in_specs=[pl.BlockSpec(memory_space=pltpu.SMEM)] + [hbm] * 6,
        out_specs=[vmem, vmem],
        out_shape=[shape, shape],
        scratch_shapes=[
            pltpu.VMEM((2,) + shares, own.dtype),
            pltpu.VMEM((2, 2) + shares, own.dtype),
            pltpu.VMEM((2,) + feats.shape, feats.dtype),
            pltpu.VMEM((depth, TOGETHER * cols), own.dtype),
            pltpu.VMEM((depth, TOGETHER * cols), own.dtype),
            pltpu.VMEM((depth, chan), jnp.float32),
            pltpu.SemaphoreType.DMA((4,)),
            pltpu.SemaphoreType.DMA((2, rows_dev // TOGETHER)),
        ],
        compiler_params=pltpu.CompilerParams(vmem_limit_bytes=24 << 20),
        cost_estimate=pl.CostEstimate(
            flops=4 * depth * rows_dev * cols * chan,
            transcendentals=0,
            bytes_accessed=4 * feats.size + 4 * depth * chan,
        ),
        name="kernel_grad",
    )(
        bits,
        split(own),
        split(pair),
        split(far[0]),
        split(far[1]),
        pltpu.with_memory_space_constraint(feats, pltpu.HBM),
        feats_far,
    )
    view = lambda a: a.reshape(2, 9, lanes, chan)
    return view(keep), view(send)


def input_grad_body(together, first_row, half_ref, *refs):
    sources, weights, (out, own, pairs, taps, sems) = refs[:8], refs[8], refs[-5:]
    turn = pl.program_id(0)
    turns = pl.num_programs(0)
    rows, half_out, cols = own.shape[2:]
    half = half_ref[0]
    count = weights.shape[0]
    targets = [own.at[at] for at in range(2)] + [pairs.at[at] for at in range(6)]
    loads = [
        pltpu.make_async_copy(source.at[:, pl.ds(first_row, rows)], target, sems.at[at])
        for at, (source, target) in enumerate(zip(sources, targets))
    ]

    def build(branch, at_turn):
        for row in range(together):
            at_row = at_turn * together + row
            for which in range(2):
                place = half if which == 0 else 1 - half
                for row_step in range(3):
                    if row_step == 1:
                        tile = own[which, branch, at_row]
                    else:
                        tile = pairs[2 * branch + which, row_step // 2, at_row]
                    turned = tile.T
                    for step in (-1, 0, 1):
                        tap = row_step * 3 + step + 1
                        at = pl.multiple_of((tap * 2 + place) * half_out, half_out)
                        taps[branch, row * cols : (row + 1) * cols, pl.ds(at, half_out)] = moved(
                            turned, step * RATES[branch], 0
                        )

    @pl.when(turn == 0)
    def _():
        for load in loads:
            load.start()
        for load in loads:
            load.wait()
        build(0, 0)

    total = None
    for branch in range(count):
        part = jnp.dot(taps[branch], weights[branch], preferred_element_type=jnp.float32)
        total = part if total is None else total + part
        if branch + 1 < count:
            build(branch + 1, turn)
        else:
            build(0, jnp.minimum(turn + 1, turns - 1))
    out[...] = total.astype(out.dtype)


def input_grad(half, own, own_other, pairs, weights, first_row, rows, before, together=1):
    rows_dev, half_out, cols = own.shape[1:]
    count, depth, chan = weights.shape
    vmem = pl.BlockSpec(memory_space=pltpu.VMEM)
    hbm = pl.BlockSpec(memory_space=pl.ANY)
    operands = (half, own, own_other, *pairs, weights) + before
    return pl.pallas_call(
        functools.partial(input_grad_body, together, first_row),
        grid=(rows // together,),
        in_specs=[pl.BlockSpec(memory_space=pltpu.SMEM)]
        + [hbm] * 8
        + [vmem]
        + [hbm] * len(before),
        out_specs=pl.BlockSpec(
            (together * cols, chan), lambda turn: (turn + first_row // together, 0)
        ),
        input_output_aliases={10: 0} if before else {},
        scratch_shapes=[
            pltpu.VMEM((2, count, rows, half_out, cols), own.dtype),
            pltpu.VMEM((2 * count, 2, rows, half_out, cols), own.dtype),
            pltpu.VMEM((count, together * cols, depth), own.dtype),
            pltpu.SemaphoreType.DMA((8,)),
        ],
        out_shape=jax.ShapeDtypeStruct((rows_dev * cols, chan), jnp.bfloat16),
        compiler_params=pltpu.CompilerParams(vmem_limit_bytes=24 << 20),
        cost_estimate=pl.CostEstimate(
            flops=2 * rows * cols * count * depth * chan,
            transcendentals=0,
            bytes_accessed=2 * weights.size + 2 * rows * cols * chan,
        ),
        name="input_grad",
    )(*operands)


def prepared_body(grad_out, pre_act, feats, masked, powers, feat_sums, mask_sums):
    turn = pl.program_id(0)

    @pl.when(turn == 0)
    def _():
        feat_sums[...] = jnp.zeros_like(feat_sums)
        mask_sums[...] = jnp.zeros_like(mask_sums)

    grad = grad_out[...]
    kept = jnp.where(pre_act[...] > 0, grad, jnp.zeros_like(grad))
    masked[...] = kept
    wide = kept[:, 0].astype(jnp.float32)
    mask_sums[...] += wide * wide
    wide = feats[0].astype(jnp.float32)
    feat_sums[...] += jnp.sum((wide * wide).reshape(-1, 8, wide.shape[1]), axis=0)

    @pl.when(turn == pl.num_programs(0) - 1)
    def _():
        feat_power = jnp.max(jnp.sum(feat_sums[...], axis=0, keepdims=True))
        mask_power = jnp.max(jnp.sum(mask_sums[...], axis=2, keepdims=True))
        upper = lax.broadcasted_iota(jnp.int32, powers.shape, 0) < 4
        powers[...] = jnp.where(upper, feat_power, mask_power)


def prepared(grad_out, pre_act, features):
    count, rows_dev, share, cols = grad_out.shape
    chan = features.shape[2]
    block = pl.BlockSpec((count, 1, share, cols), lambda turn: (0, turn, 0, 0))
    return pl.pallas_call(
        prepared_body,
        grid=(rows_dev,),
        in_specs=[block, block, pl.BlockSpec((1, cols, chan), lambda turn: (turn, 0, 0))],
        out_specs=[block, pl.BlockSpec((8, 128), lambda turn: (0, 0))],
        out_shape=[
            jax.ShapeDtypeStruct(grad_out.shape, grad_out.dtype),
            jax.ShapeDtypeStruct((8, 128), jnp.float32),
        ],
        scratch_shapes=[
            pltpu.VMEM((8, chan), jnp.float32),
            pltpu.VMEM((count, share, cols), jnp.float32),
        ],
        compiler_params=pltpu.CompilerParams(vmem_limit_bytes=16 << 20),
        name="prepared",
    )(*(pltpu.with_memory_space_constraint(a, pltpu.HBM) for a in (grad_out, pre_act, features)))


def partial_bound(both):
    upper = lax.broadcasted_iota(jnp.int32, both.shape, 0) < 4
    other = swapped(both, "chan", 1)
    both = jnp.where(upper, both, jnp.maximum(both, other))
    bit = 1
    while bit < lax.axis_size("rows"):
        both = both + swapped(both, "rows", bit)
        bit *= 2
    return jnp.maximum(jnp.sqrt(both[0, 0]) * jnp.sqrt(both[4, 0]) * 1.01, 1e-30)


def shards(features, grad_out, pre_act, weights):
    rows_dev, cols, local_chan = features.shape
    out_chan = weights.shape[2]
    strips = lax.axis_size("rows")
    lanes = out_chan // strips
    place = lax.axis_index("rows")
    half = lax.axis_index("chan")
    core, y_at, z_low, z_high = place % 2, place // 2 % 2, place // 4 % 2, place // 8
    bits = jnp.stack([core, y_at]).astype(jnp.int32)
    half_arg = half.astype(jnp.int32).reshape(1)
    kernels = weights.reshape(3, 9 * out_chan, local_chan)
    masked, powers = prepared(grad_out, pre_act, features)
    feats = features.reshape(rows_dev * cols, local_chan)
    feats_far = swapped(feats, "rows", 1)
    bound = partial_bound(powers)
    grow, shrink = 32000.0 / bound, bound / 32000.0

    own = [masked, swapped(masked, "chan", 1)]
    pieces = []
    for branch, dilation in enumerate(RATES):
        pieces.append(fetch(masked[branch], 1, dilation) + fetch(masked[branch], -1, dilation))
    own_far = [swapped(own[0], "rows", 1), None]
    pairs, pairs_far = [[None] * 3, [None] * 3], [[None] * 3, [None] * 3]

    def join(branch, gate):
        pair = joined(after(pieces[branch], gate)).reshape((2,) + masked.shape[1:])
        pair = lax.optimization_barrier(pair)
        pairs[1][branch] = swapped(pair, "chan", 1)
        pairs[0][branch] = pair
        pairs_far[0][branch] = swapped(pair, "rows", 1)

    def share_with_core(branch, gate):
        if branch == 0:
            own_far[1] = swapped(after(own[1], gate), "rows", 1)
        pairs_far[1][branch] = swapped(after(pairs[1][branch], gate), "rows", 1)


    def pack(values):
        return (values * grow).astype(jnp.float16)

    def unpack(values):
        return values.astype(jnp.float32) * shrink

    steps = [(share, branch) for share in range(2) for branch in range(3)]
    state, result = {}, {}

    def first_stage(at, gate):
        share, branch = steps[at]
        keep, send = kernel_grad(
            after(bits, gate),
            (own[share], pairs[share][branch]),
            (own_far[share], pairs_far[share][branch]),
            feats,
            feats_far,
            branch,
            lanes,
        )
        send = pack(send)
        state[at] = (keep, swapped(send, "rows", 2))
        return [send, keep]

    def second_stage(at, gate):
        keep, got = after(state[at], gate)
        total = keep + unpack(got)
        send = pack(lax.dynamic_index_in_dim(total, 1 - z_low, 0, keepdims=False))
        keep = lax.dynamic_index_in_dim(total, z_low, 0, keepdims=False)
        state[at] = (keep, swapped(send, "rows", 4))
        return [send, keep]

    def third_stage(at, gate):
        share = steps[at][0]
        keep, got = after(state[at], gate)
        total = keep + unpack(got)
        pairs = [
            (row * 2 + chan, (row ^ 8) * 2 + chan)
            for row in range(strips)
            for chan in range(2)
            if row // 8 != (chan if share == 0 else 1 - chan)
        ]
        send = pack(total)
        state[at] = (total, lax.ppermute(send, ("rows", "chan"), pairs))
        return [send, total]

    def last_stage(at, gate):
        keep, got = after(state[at], gate)
        result[at] = keep + unpack(got)
        return [result[at]]

    row_parts = []
    first_row = 0

    def rows_of_input_grad(count, gate):
        nonlocal first_row
        flat = [pairs[share][branch] for branch in range(3) for share in range(2)]
        part = input_grad(
            after(half_arg, gate),
            own[0],
            own[1],
            flat,
            kernels,
            first_row,
            count,
            tuple(row_parts[-1:]),
        )
        row_parts.append(part)
        first_row += count
        return [row_parts[-1]]

    join(0, [])
    join(1, [])
    gate = first_stage(0, [])
    join(2, gate)
    gate = first_stage(1, gate)
    ready = first_stage(2, gate)
    share_with_core(0, ready)
    gate = ready + second_stage(0, ready)
    ready = first_stage(3, gate)
    share_with_core(1, ready)
    gate = ready + second_stage(1, ready)
    ready = first_stage(4, gate)
    share_with_core(2, ready)
    gate = ready + second_stage(2, ready) + third_stage(0, ready) + second_stage(3, ready)
    ready = first_stage(5, gate)
    gate = ready + third_stage(1, ready) + second_stage(4, ready)
    gate += third_stage(2, ready) + third_stage(3, ready)
    ready = rows_of_input_grad(GRAD_PARTS[0], gate)
    gate = ready + second_stage(5, ready) + third_stage(4, ready)
    ready = rows_of_input_grad(GRAD_PARTS[1], gate)
    gate = ready + third_stage(5, ready)
    ready = rows_of_input_grad(GRAD_PARTS[2], gate)
    for at in range(6):
        last_stage(at, ready)
    mine = z_high == half
    grad_weight = jnp.stack(
        [jnp.where(mine, result[branch], result[3 + branch]) for branch in range(3)]
    )
    grad_input = row_parts[-1].reshape(rows_dev, cols, local_chan)
    return grad_input, grad_weight * grad_scale


def general(features, grad_out, pre_act, weights):
    rows_dev, cols, local_chan = features.shape
    out_chan = weights.shape[2]
    masked = grad_out * (pre_act > 0).astype(jnp.bfloat16)
    own_rows = lax.all_gather(masked, "chan", axis=2, tiled=True)
    kernels = weights.reshape(3, 9 * out_chan, local_chan)
    grad_input = jnp.zeros((rows_dev, cols, local_chan), jnp.float32)
    kernel_list = []
    for branch, dilation in enumerate(RATES):
        tap_list = []
        for row_step in (-1, 0, 1):
            rows = own_rows[branch]
            if row_step:
                rows = jnp.concatenate(fetch(rows, -row_step, dilation))
            padded = jnp.pad(rows, ((0, 0), (0, 0), (dilation, dilation)))
            for col_step in (-1, 0, 1):
                cols_at = dilation - col_step * dilation
                tap_list.append(padded[:, :, cols_at : cols_at + cols])
        stacked_taps = jnp.concatenate(tap_list, axis=1)
        grad_input = grad_input + jnp.einsum(
            "rkc,ki->rci", stacked_taps, kernels[branch], preferred_element_type=jnp.float32
        )
        kernel_list.append(
            jnp.einsum("rkc,rci->ki", stacked_taps, features, preferred_element_type=jnp.float32)
        )
    partial_grad = jnp.stack(kernel_list, axis=0).reshape(3, 9, out_chan, local_chan)
    summed = lax.psum_scatter(partial_grad, "rows", scatter_dimension=2, tiled=True)
    return (grad_input.astype(jnp.bfloat16), summed * grad_scale)


def solution(mesh):
    in_specs = (
        P("rows", None, "chan"),
        P(None, "rows", "chan", None),
        P(None, "rows", "chan", None),
        P(None, None, None, "chan"),
    )
    out_specs = (P("rows", None, "chan"), P(None, None, "rows", "chan"))
    fast = mesh.shape["rows"] == 16 and mesh.shape["chan"] == 2
    if not fast:
        return jax.shard_map(
            general, mesh=mesh, in_specs=in_specs, out_specs=out_specs, check_vma=False
        )

    return jax.shard_map(shards, mesh=mesh, in_specs=in_specs, out_specs=out_specs, check_vma=False)
```

```python
import functools

import jax
import jax.numpy as jnp
from jax import lax
from jax.experimental import pallas as pl
from jax.experimental.pallas import tpu as pltpu
from jax.sharding import PartitionSpec as P

RATES = (12, 24, 36)
grad_scale = 0.00390625
TOGETHER = 2
GRAD_PARTS = (2, 3, 3)


def passed_along(array, axis, by):
    count = lax.axis_size(axis)
    pairs = [(i, i + by) for i in range(count) if 0 <= i + by < count]
    return lax.ppermute(array, axis, pairs)


def swapped(array, axis, bit):
    count = lax.axis_size(axis)
    return lax.ppermute(array, axis, [(i, i ^ bit) for i in range(count)])


def row_pieces(dilation, side, rows_dev):
    start_strip = side * dilation // rows_dev
    remainder = side * dilation % rows_dev
    if remainder == 0:
        return [(start_strip, 0, rows_dev)]
    return [(start_strip, remainder, rows_dev), (start_strip + 1, 0, remainder)]


def fetch(source, side, dilation):
    return [
        passed_along(source[low:high], "rows", -strip)
        for strip, low, high in row_pieces(dilation, side, source.shape[0])
    ]


def after(values, gate):
    return lax.optimization_barrier((values, gate))[0]


def moved(tile, shift, axis):
    if shift == 0:
        return tile
    size = tile.shape[axis]
    at = lax.broadcasted_iota(jnp.int32, tile.shape, axis)
    keep = at >= shift if shift > 0 else at < size + shift
    return jnp.where(keep, pltpu.roll(tile, shift % size, axis), jnp.zeros_like(tile))


def joined(pieces):
    if len({piece.shape for piece in pieces}) == 1:
        stacked = jnp.stack(pieces)
        return stacked.reshape((-1,) + stacked.shape[2:])
    return jnp.concatenate(pieces)


def kernel_grad_body(branch, dilation, bits_ref, own_hbm, pair_hbm, own_far_hbm, pair_far_hbm,
                     feats_hbm, feats_far_hbm, keep_out, send_out, own, pair, feats, taps_near,
                     taps_far, sums, row_sems, feat_sems):
    _, rows_dev, low, _, _, lanes, cols = own.shape
    core, first = bits_ref[0], bits_ref[1]
    turns = rows_dev // TOGETHER
    span = TOGETHER * cols
    near_loads = (
        pltpu.make_async_copy(own_hbm.at[branch], own.at[0], row_sems.at[0]),
        pltpu.make_async_copy(pair_hbm, pair.at[0], row_sems.at[1]),
    )
    far_loads = (
        pltpu.make_async_copy(own_far_hbm.at[branch], own.at[1], row_sems.at[2]),
        pltpu.make_async_copy(pair_far_hbm, pair.at[1], row_sems.at[3]),
    )

    def feat_load(which, turn):
        rows = pl.ds(pl.multiple_of(turn * span, span), span)
        source = (feats_hbm, feats_far_hbm)[which]
        return pltpu.make_async_copy(
            source.at[rows], feats.at[which, rows], feat_sems.at[which, turn]
        )

    for load in near_loads:
        load.start()
    feat_load(0, 0).start()
    for load in near_loads:
        load.wait()
    for load in far_loads:
        load.start()
    feat_load(1, 0).start()
    for turn in range(1, turns):
        feat_load(0, turn).start()
        feat_load(1, turn).start()

    def build(which, turn, target):
        for row in range(TOGETHER):
            at_row = turn * TOGETHER + row
            for part in range(2):
                bit = first if part == 0 else 1 - first
                for row_step in range(3):
                    for group in range(low):
                        place = (group, bit, core)
                        if row_step == 1:
                            tile = own[(which, at_row) + place]
                        else:
                            tile = pair[(which, row_step // 2, at_row) + place]
                        for step in (-1, 0, 1):
                            tap = row_step * 3 + step + 1
                            at = ((part * low + group) * 9 + tap) * lanes
                            target[at : at + lanes, row * cols : (row + 1) * cols] = moved(
                                tile, step * dilation, 1
                            )

    build(0, 0, taps_near)
    sums[...] = jnp.zeros_like(sums)
    for load in far_loads:
        load.wait()

    def step(turn, carry):
        rows = pl.ds(pl.multiple_of(turn * span, span), span)
        feat_load(0, turn).wait()
        feat_load(1, turn).wait()
        sums[...] += jnp.dot(
            taps_near[...], feats[0, rows, :], preferred_element_type=jnp.float32
        )
        build(1, turn, taps_far)
        sums[...] += jnp.dot(taps_far[...], feats[1, rows, :], preferred_element_type=jnp.float32)
        build(0, jnp.minimum(turn + 1, turns - 1), taps_near)
        return carry

    lax.fori_loop(0, turns, step, 0)
    size = keep_out.shape[0]
    keep_out[...] = sums[:size]
    send_out[...] = sums[size:]


def kernel_grad(bits, near, far, feats, feats_far, branch, lanes):
    own, pair = near
    rows_dev, half_out, cols = own.shape[1:]
    chan = feats.shape[1]
    vmem = pl.BlockSpec(memory_space=pltpu.VMEM)
    hbm = pl.BlockSpec(memory_space=pl.ANY)
    depth = 9 * half_out // 2
    shares = (rows_dev, 2, 2, 2, lanes, cols)
    split = lambda a: a.reshape((a.shape[0],) + shares)
    shape = jax.ShapeDtypeStruct((depth // 2, chan), jnp.float32)
    keep, send = pl.pallas_call(
        functools.partial(kernel_grad_body, branch, RATES[branch]),
        in_specs=[pl.BlockSpec(memory_space=pltpu.SMEM)] + [hbm] * 6,
        out_specs=[vmem, vmem],
        out_shape=[shape, shape],
        scratch_shapes=[
            pltpu.VMEM((2,) + shares, own.dtype),
            pltpu.VMEM((2, 2) + shares, own.dtype),
            pltpu.VMEM((2,) + feats.shape, feats.dtype),
            pltpu.VMEM((depth, TOGETHER * cols), own.dtype),
            pltpu.VMEM((depth, TOGETHER * cols), own.dtype),
            pltpu.VMEM((depth, chan), jnp.float32),
            pltpu.SemaphoreType.DMA((4,)),
            pltpu.SemaphoreType.DMA((2, rows_dev // TOGETHER)),
        ],
        compiler_params=pltpu.CompilerParams(vmem_limit_bytes=24 << 20),
        cost_estimate=pl.CostEstimate(
            flops=4 * depth * rows_dev * cols * chan,
            transcendentals=0,
            bytes_accessed=4 * feats.size + 4 * depth * chan,
        ),
        name="kernel_grad",
    )(
        bits,
        split(own),
        split(pair),
        split(far[0]),
        split(far[1]),
        pltpu.with_memory_space_constraint(feats, pltpu.HBM),
        feats_far,
    )
    view = lambda a: a.reshape(2, 9, lanes, chan)
    return view(keep), view(send)


def input_grad_body(together, first_row, half_ref, *refs):
    sources, weights, (out, own, pairs, taps, sems) = refs[:8], refs[8], refs[-5:]
    turn = pl.program_id(0)
    turns = pl.num_programs(0)
    rows, half_out, cols = own.shape[2:]
    half = half_ref[0]
    count = weights.shape[0]
    targets = [own.at[at] for at in range(2)] + [pairs.at[at] for at in range(6)]
    loads = [
        pltpu.make_async_copy(source.at[:, pl.ds(first_row, rows)], target, sems.at[at])
        for at, (source, target) in enumerate(zip(sources, targets))
    ]

    def build(branch, at_turn):
        for row in range(together):
            at_row = at_turn * together + row
            for which in range(2):
                place = half if which == 0 else 1 - half
                for row_step in range(3):
                    if row_step == 1:
                        tile = own[which, branch, at_row]
                    else:
                        tile = pairs[2 * branch + which, row_step // 2, at_row]
                    turned = tile.T
                    for step in (-1, 0, 1):
                        tap = row_step * 3 + step + 1
                        at = pl.multiple_of((tap * 2 + place) * half_out, half_out)
                        taps[branch, row * cols : (row + 1) * cols, pl.ds(at, half_out)] = moved(
                            turned, step * RATES[branch], 0
                        )

    @pl.when(turn == 0)
    def _():
        for load in loads:
            load.start()
        for load in loads:
            load.wait()
        build(0, 0)

    total = None
    for branch in range(count):
        part = jnp.dot(taps[branch], weights[branch], preferred_element_type=jnp.float32)
        total = part if total is None else total + part
        if branch + 1 < count:
            build(branch + 1, turn)
        else:
            build(0, jnp.minimum(turn + 1, turns - 1))
    out[...] = total.astype(out.dtype)


def input_grad(half, own, own_other, pairs, weights, first_row, rows, before, together=1):
    rows_dev, half_out, cols = own.shape[1:]
    count, depth, chan = weights.shape
    vmem = pl.BlockSpec(memory_space=pltpu.VMEM)
    hbm = pl.BlockSpec(memory_space=pl.ANY)
    operands = (half, own, own_other, *pairs, weights) + before
    return pl.pallas_call(
        functools.partial(input_grad_body, together, first_row),
        grid=(rows // together,),
        in_specs=[pl.BlockSpec(memory_space=pltpu.SMEM)]
        + [hbm] * 8
        + [vmem]
        + [hbm] * len(before),
        out_specs=pl.BlockSpec(
            (together * cols, chan), lambda turn: (turn + first_row // together, 0)
        ),
        input_output_aliases={10: 0} if before else {},
        scratch_shapes=[
            pltpu.VMEM((2, count, rows, half_out, cols), own.dtype),
            pltpu.VMEM((2 * count, 2, rows, half_out, cols), own.dtype),
            pltpu.VMEM((count, together * cols, depth), own.dtype),
            pltpu.SemaphoreType.DMA((8,)),
        ],
        out_shape=jax.ShapeDtypeStruct((rows_dev * cols, chan), jnp.bfloat16),
        compiler_params=pltpu.CompilerParams(vmem_limit_bytes=24 << 20),
        cost_estimate=pl.CostEstimate(
            flops=2 * rows * cols * count * depth * chan,
            transcendentals=0,
            bytes_accessed=2 * weights.size + 2 * rows * cols * chan,
        ),
        name="input_grad",
    )(*operands)


def prepared_body(grad_out, pre_act, feats, masked, powers, feat_sums, mask_sums):
    turn = pl.program_id(0)

    @pl.when(turn == 0)
    def _():
        feat_sums[...] = jnp.zeros_like(feat_sums)
        mask_sums[...] = jnp.zeros_like(mask_sums)

    grad = grad_out[...]
    kept = jnp.where(pre_act[...] > 0, grad, jnp.zeros_like(grad))
    masked[...] = kept
    for row in range(kept.shape[1]):
        wide = kept[:, row].astype(jnp.float32)
        mask_sums[...] += wide * wide
        wide = feats[row].astype(jnp.float32)
        feat_sums[...] += jnp.sum((wide * wide).reshape(-1, 8, wide.shape[1]), axis=0)

    @pl.when(turn == pl.num_programs(0) - 1)
    def _():
        feat_power = jnp.max(jnp.sum(feat_sums[...], axis=0, keepdims=True))
        mask_power = jnp.max(jnp.sum(mask_sums[...], axis=2, keepdims=True))
        upper = lax.broadcasted_iota(jnp.int32, powers.shape, 0) < 4
        powers[...] = jnp.where(upper, feat_power, mask_power)


def prepared(grad_out, pre_act, features):
    count, rows_dev, share, cols = grad_out.shape
    chan = features.shape[2]
    block = pl.BlockSpec((count, 2, share, cols), lambda turn: (0, turn, 0, 0))
    return pl.pallas_call(
        prepared_body,
        grid=(rows_dev // 2,),
        in_specs=[block, block, pl.BlockSpec((2, cols, chan), lambda turn: (turn, 0, 0))],
        out_specs=[block, pl.BlockSpec((8, 128), lambda turn: (0, 0))],
        out_shape=[
            jax.ShapeDtypeStruct(grad_out.shape, grad_out.dtype),
            jax.ShapeDtypeStruct((8, 128), jnp.float32),
        ],
        scratch_shapes=[
            pltpu.VMEM((8, chan), jnp.float32),
            pltpu.VMEM((count, share, cols), jnp.float32),
        ],
        compiler_params=pltpu.CompilerParams(vmem_limit_bytes=16 << 20),
        name="prepared",
    )(*(pltpu.with_memory_space_constraint(a, pltpu.HBM) for a in (grad_out, pre_act, features)))


def start_bound(both):
    upper = lax.broadcasted_iota(jnp.int32, both.shape, 0) < 4
    other = swapped(both, "chan", 1)
    return jnp.where(upper, both, jnp.maximum(both, other))


def sent_bound(both, bit):
    return both, swapped(both, "rows", bit)


def finished_bound(both):
    return jnp.maximum(jnp.sqrt(both[0, 0]) * jnp.sqrt(both[4, 0]) * 1.01, 1e-30)


def shards(features, grad_out, pre_act, weights):
    rows_dev, cols, local_chan = features.shape
    out_chan = weights.shape[2]
    strips = lax.axis_size("rows")
    lanes = out_chan // strips
    place = lax.axis_index("rows")
    half = lax.axis_index("chan")
    core, y_at, z_low, z_high = place % 2, place // 2 % 2, place // 4 % 2, place // 8
    bits = jnp.stack([core, y_at]).astype(jnp.int32)
    half_arg = half.astype(jnp.int32).reshape(1)
    kernels = weights.reshape(3, 9 * out_chan, local_chan)
    masked, powers = prepared(grad_out, pre_act, features)
    feats = features.reshape(rows_dev * cols, local_chan)
    feats_far = swapped(feats, "rows", 1)
    both = start_bound(powers)
    for bit in (1, 2):
        both = sum(sent_bound(both, bit))
    both = sent_bound(both, 4)
    scales = {}

    own = [masked, swapped(masked, "chan", 1)]
    pieces = []
    for branch, dilation in enumerate(RATES):
        pieces.append(fetch(masked[branch], 1, dilation) + fetch(masked[branch], -1, dilation))
    own_far = [swapped(own[0], "rows", 1), None]
    pairs, pairs_far = [[None] * 3, [None] * 3], [[None] * 3, [None] * 3]

    def join(branch, gate):
        pair = joined(after(pieces[branch], gate)).reshape((2,) + masked.shape[1:])
        pair = lax.optimization_barrier(pair)
        pairs[1][branch] = swapped(pair, "chan", 1)
        pairs[0][branch] = pair
        pairs_far[0][branch] = swapped(pair, "rows", 1)

    def share_with_core(branch, gate):
        if branch == 0:
            own_far[1] = swapped(after(own[1], gate), "rows", 1)
        pairs_far[1][branch] = swapped(after(pairs[1][branch], gate), "rows", 1)


    def pack(values):
        return (values * scales["grow"]).astype(jnp.float16)

    def unpack(values):
        return values.astype(jnp.float32) * scales["shrink"]

    steps = [(share, branch) for share in range(2) for branch in range(3)]
    state, result = {}, {}

    def first_stage(at, gate):
        share, branch = steps[at]
        keep, send = kernel_grad(
            after(bits, gate),
            (own[share], pairs[share][branch]),
            (own_far[share], pairs_far[share][branch]),
            feats,
            feats_far,
            branch,
            lanes,
        )
        state[at] = (keep, send)
        return [send, keep] if at < 2 else first_send(at)

    def first_send(at):
        keep, send = state[at]
        send = pack(send)
        state[at] = (keep, swapped(send, "rows", 2))
        return [send, keep]

    def second_stage(at, gate):
        keep, got = after(state[at], gate)
        total = keep + unpack(got)
        send = pack(lax.dynamic_index_in_dim(total, 1 - z_low, 0, keepdims=False))
        keep = lax.dynamic_index_in_dim(total, z_low, 0, keepdims=False)
        state[at] = (keep, swapped(send, "rows", 4))
        return [send, keep]

    def third_stage(at, gate):
        share = steps[at][0]
        keep, got = after(state[at], gate)
        total = keep + unpack(got)
        pairs = [
            (row * 2 + chan, (row ^ 8) * 2 + chan)
            for row in range(strips)
            for chan in range(2)
            if row // 8 != (chan if share == 0 else 1 - chan)
        ]
        send = pack(total)
        state[at] = (total, lax.ppermute(send, ("rows", "chan"), pairs))
        return [send, total]

    def last_stage(at, gate):
        keep, got = after(state[at], gate)
        result[at] = keep + unpack(got)
        return [result[at]]

    row_parts = []
    first_row = 0

    def rows_of_input_grad(count, gate):
        nonlocal first_row
        flat = [pairs[share][branch] for branch in range(3) for share in range(2)]
        part = input_grad(
            after(half_arg, gate),
            own[0],
            own[1],
            flat,
            kernels,
            first_row,
            count,
            tuple(row_parts[-1:]),
        )
        row_parts.append(part)
        first_row += count
        return [row_parts[-1]]

    join(0, [])
    join(1, [])
    gate = first_stage(0, [])
    join(2, gate)
    both = sent_bound(sum(after(both, gate)), 8)
    gate = first_stage(1, gate + [both[0]])
    bound = finished_bound(sum(after(both, gate)))
    scales.update(grow=32000.0 / bound, shrink=bound / 32000.0)
    gate = first_send(0) + first_send(1)
    ready = first_stage(2, gate)
    share_with_core(0, ready)
    gate = ready + second_stage(0, ready)
    ready = first_stage(3, gate)
    share_with_core(1, ready)
    gate = ready + second_stage(1, ready)
    ready = first_stage(4, gate)
    share_with_core(2, ready)
    gate = ready + second_stage(2, ready) + third_stage(0, ready) + second_stage(3, ready)
    ready = first_stage(5, gate)
    gate = ready + third_stage(1, ready) + second_stage(4, ready)
    gate += third_stage(2, ready)
    ready = rows_of_input_grad(GRAD_PARTS[0], gate)
    gate = ready + third_stage(3, ready) + second_stage(5, ready) + third_stage(4, ready)
    ready = rows_of_input_grad(GRAD_PARTS[1], gate)
    gate = ready + third_stage(5, ready)
    ready = rows_of_input_grad(GRAD_PARTS[2], gate)
    for at in range(6):
        last_stage(at, ready)
    mine = z_high == half
    grad_weight = jnp.stack(
        [jnp.where(mine, result[branch], result[3 + branch]) for branch in range(3)]
    )
    grad_input = row_parts[-1].reshape(rows_dev, cols, local_chan)
    return grad_input, grad_weight * grad_scale


def general(features, grad_out, pre_act, weights):
    rows_dev, cols, local_chan = features.shape
    out_chan = weights.shape[2]
    masked = grad_out * (pre_act > 0).astype(jnp.bfloat16)
    own_rows = lax.all_gather(masked, "chan", axis=2, tiled=True)
    kernels = weights.reshape(3, 9 * out_chan, local_chan)
    grad_input = jnp.zeros((rows_dev, cols, local_chan), jnp.float32)
    kernel_list = []
    for branch, dilation in enumerate(RATES):
        tap_list = []
        for row_step in (-1, 0, 1):
            rows = own_rows[branch]
            if row_step:
                rows = jnp.concatenate(fetch(rows, -row_step, dilation))
            padded = jnp.pad(rows, ((0, 0), (0, 0), (dilation, dilation)))
            for col_step in (-1, 0, 1):
                cols_at = dilation - col_step * dilation
                tap_list.append(padded[:, :, cols_at : cols_at + cols])
        stacked_taps = jnp.concatenate(tap_list, axis=1)
        grad_input = grad_input + jnp.einsum(
            "rkc,ki->rci", stacked_taps, kernels[branch], preferred_element_type=jnp.float32
        )
        kernel_list.append(
            jnp.einsum("rkc,rci->ki", stacked_taps, features, preferred_element_type=jnp.float32)
        )
    partial_grad = jnp.stack(kernel_list, axis=0).reshape(3, 9, out_chan, local_chan)
    summed = lax.psum_scatter(partial_grad, "rows", scatter_dimension=2, tiled=True)
    return (grad_input.astype(jnp.bfloat16), summed * grad_scale)


def solution(mesh):
    in_specs = (
        P("rows", None, "chan"),
        P(None, "rows", "chan", None),
        P(None, "rows", "chan", None),
        P(None, None, None, "chan"),
    )
    out_specs = (P("rows", None, "chan"), P(None, None, "rows", "chan"))
    fast = mesh.shape["rows"] == 16 and mesh.shape["chan"] == 2
    if not fast:
        return jax.shard_map(
            general, mesh=mesh, in_specs=in_specs, out_specs=out_specs, check_vma=False
        )

    return jax.shard_map(shards, mesh=mesh, in_specs=in_specs, out_specs=out_specs, check_vma=False)
```
